32 devices in a mesh: grp: 4 (over y, x), mem: 8 (over z, core).
Axes of the slice: x: 2, y: 2, z: 4, core: 2. Of those that a mesh axis runs over, the one named last changes fastest.
Arguments:
- user_rows: bfloat16 [4096, 2048], P(('grp', 'mem')), may hold values from -6 to 6
- projection: bfloat16 [2048, 2048], replicated, may hold values from -0.125 to 0.125
- item_table: bfloat16 [8192, 2048], P(('grp', 'mem')), may hold values from -8 to 8
- positive: int32 [4096], P(('grp', 'mem')), may hold values from 0 to 8191, as said below
- negatives: int32 [4, 1024], P(None, ('grp', 'mem')), may hold values from 0 to 8191, as said below
Outputs:
- user_grad: bfloat16 [4096, 2048], P(('grp', 'mem'))
- item_grad: float32 [8192, 2048], P(('grp', 'mem'))
The draws below stay inside these ranges and needn't reach their ends.
Inputs may be any that keep to these rules, and one draw needn't show every extreme that they name: `positive`: owner o (grp-major order over grp and mem) holds item rows o * 256 to (o + 1) * 256 - 1. Among the 128 rows of any one device, at most 16 positives lie with any one owner, and one owner receives exactly 16 from every device. `negatives`: in every group, negative j is one of the item rows of owner j // 32.
All inputs are finite; a program needn't handle non-finite values.
Results may differ from the reference program's by a relative error of at most 0.0075.
Values may be sent and summed in bfloat16 or wider, within the bound.
No kernel may reach another device: no remote copies, remote signals or barrier semaphores. Data moves between devices by JAX's collectives and lax.ppermute only.
A program may use at most 64 MiB of HBM per device.

```python
import math
import jax
import jax.numpy as jnp
from jax import lax

D = 2048
U_DEV = 128
ITEMS = 8192
NEG = 1024
USERS = 4096
N_GRP = 4
N_MEM = 8


def draw_item_table(key, part):
    key_base = jax.random.fold_in(key, 0)
    base_rows = jax.random.truncated_normal(key_base, -4.0, 4.0, (ITEMS, D), jnp.float32)
    return base_rows.astype(jnp.bfloat16)


def draw_positive(key, part):
    owners = N_GRP * N_MEM
    capacity = 4 * U_DEV // owners
    own_rows = ITEMS // owners
    key_hot, key_start, key_order, key_offset = jax.random.split(key, 4)
    hot_owner = jax.random.randint(key_hot, (), 0, owners)
    starts = jax.random.randint(key_start, (owners, 1), 0, owners - 1)
    step_index = jnp.arange(U_DEV, dtype=jnp.int32)[None, :]
    other_owner = (starts + step_index - capacity) % (owners - 1)
    other_owner = other_owner + (other_owner >= hot_owner).astype(jnp.int32)
    owner_index = jnp.where(step_index < capacity, hot_owner, other_owner)
    scores = jax.random.randint(key_order, (owners, U_DEV), 0, 1 << 20) * U_DEV + step_index
    row_order = jnp.argsort(scores, axis=1, stable=True)
    owner_index = jnp.take_along_axis(owner_index, row_order, axis=1)
    offsets = jax.random.randint(key_offset, (owners, U_DEV), 0, own_rows)
    return (owner_index * own_rows + offsets).reshape(-1).astype(jnp.int32)


def draw_negatives(key, part):
    owners = N_GRP * N_MEM
    own_rows = ITEMS // owners
    column = jnp.arange(NEG, dtype=jnp.int32)[None, :]
    offsets = jax.random.randint(key, (N_GRP, NEG), 0, own_rows)
    return (column // (NEG // owners) * own_rows + offsets).astype(jnp.int32)


def level_of(key, shape, cuts, low, high):
    def one(dim, blocks):
        draws = jax.random.uniform(jax.random.fold_in(jax.random.fold_in(key, 6), dim), (blocks,), jnp.float32, low / len(cuts), high / len(cuts))
        return jnp.repeat(jnp.exp(draws), shape[dim] // blocks).reshape((-1,) + (1,) * (len(shape) - dim - 1))

    gain = one(*cuts[0])
    for cut in cuts[1:]:
        gain = gain * one(*cut)
    return gain


def centred(key, extent, spread, limit, shards=(), kind=jnp.bfloat16):
    gain = level_of(key, extent, shards, -0.22, 0.18) if shards else 1.0
    values = jax.random.normal(key, extent, jnp.float32) * spread * gain
    return jnp.minimum(jnp.maximum(values, -limit), limit).astype(kind)


def setup_inputs(seed: int = 0) -> dict:
    seeds = jax.random.split(jax.random.key(seed), 6)
    user_rows = centred(seeds[0], (USERS, D), 1.0, 6.0, ((0, 32),))
    projection = centred(seeds[1], (D, D), D ** -0.5, 0.125)
    item_table = draw_item_table(jax.random.fold_in(seeds[5], 71), 0)
    positive = draw_positive(jax.random.fold_in(seeds[5], 71), 0)
    negatives = draw_negatives(jax.random.fold_in(seeds[5], 71), 0)
    return {"user_rows": user_rows, "projection": projection, "item_table": item_table, "positive": positive, "negatives": negatives}


def silu_slope(hidden):
    sigmoid_value = jax.nn.sigmoid(hidden)
    return sigmoid_value * (1.0 + hidden * (1.0 - sigmoid_value))

def reference(user_rows, projection, item_table, positive, negatives):
    score_scale = 4.0 / math.sqrt(D)
    per_group = user_rows.shape[0] // N_GRP
    item_grad = jnp.zeros(item_table.shape, jnp.float32)
    user_parts = []
    for group_index in range(N_GRP):
        user_block = user_rows[group_index * per_group:(group_index + 1) * per_group]
        pos_ids = positive[group_index * per_group:(group_index + 1) * per_group]
        neg_ids = negatives[group_index]
        hidden = jnp.dot(user_block, projection, preferred_element_type=jnp.float32)
        hidden_z = jax.nn.silu(hidden).astype(jnp.bfloat16)
        neg_table = item_table[neg_ids]
        pos_rows = item_table[pos_ids]
        neg_logits = score_scale * jnp.dot(hidden_z, neg_table.T, preferred_element_type=jnp.float32)
        pos_logit = score_scale * lax.optimization_barrier(jnp.sum(hidden_z.astype(jnp.float32) * pos_rows.astype(jnp.float32), axis=1))
        row_max = jnp.maximum(pos_logit, lax.optimization_barrier(jnp.max(neg_logits, axis=1)))
        exp_total = jnp.exp(pos_logit - row_max) + lax.optimization_barrier(jnp.sum(jnp.exp(neg_logits - row_max[:, None]), axis=1))
        log_total = row_max + jnp.log(exp_total)
        neg_prob = jnp.exp(neg_logits - log_total[:, None]).astype(jnp.bfloat16)
        pos_weight = jnp.exp(pos_logit - log_total) - 1.0
        grad_z = score_scale * (jnp.dot(neg_prob, neg_table, preferred_element_type=jnp.float32) + pos_weight[:, None] * pos_rows.astype(jnp.float32))
        grad_hidden = (grad_z * silu_slope(hidden)).astype(jnp.bfloat16)
        user_parts.append(jnp.dot(grad_hidden, projection.T, preferred_element_type=jnp.float32).astype(jnp.bfloat16))
        neg_term = score_scale * jnp.dot(neg_prob.T, hidden_z, preferred_element_type=jnp.float32)
        pos_term = (score_scale * pos_weight)[:, None] * hidden_z.astype(jnp.float32)
        item_grad = item_grad.at[neg_ids].add(neg_term).at[pos_ids].add(pos_term)
    return (jnp.concatenate(user_parts, axis=0), item_grad)
```

```python
import functools
import math

import jax
import jax.numpy as jnp
from jax import lax
from jax.experimental import pallas as pl
from jax.experimental.pallas import tpu as pltpu
from jax.sharding import PartitionSpec as P


F32 = jnp.float32
BF16 = jnp.bfloat16
VMEM_LIMIT = 60 * 1024 * 1024
VM = pl.BlockSpec(memory_space=pltpu.VMEM)
SM = pl.BlockSpec(memory_space=pltpu.SMEM)


def dot(a, b, ca=1, cb=0):
    return lax.dot_general(a, b, (((ca,), (cb,)), ((), ())), preferred_element_type=F32)


def chunk_of(width):
    return width if width < 512 else 512


def cost(flops, nbytes):
    return pl.CostEstimate(flops=int(flops), bytes_accessed=int(nbytes), transcendentals=0)


def call(kernel, outs, n_smem, args, flops, nbytes, name, aliases=None):
    return pl.pallas_call(
        kernel,
        out_shape=[jax.ShapeDtypeStruct(s, t) for s, t in outs],
        in_specs=[SM] * n_smem + [VM] * (len(args) - n_smem),
        out_specs=[VM] * len(outs),
        input_output_aliases=aliases or {},
        compiler_params=pltpu.CompilerParams(vmem_limit_bytes=VMEM_LIMIT),
        cost_estimate=cost(flops, nbytes),
        name=name,
    )(*args)


def project_kernel(x_ref, w_ref, up_ref, down_ref, hidden_ref):
    hidden = dot(x_ref[...], w_ref[...])
    hidden_ref[...] = hidden
    z = (hidden * jax.nn.sigmoid(hidden)).astype(BF16)
    half = up_ref.shape[0]
    up_ref[...] = z[:half]
    down_ref[...] = z[half:]


def project(x, w):
    rows, width = x.shape
    half = rows // 2
    tile = min(width, 256)
    col = lambda n: pl.BlockSpec((n, tile), lambda i: (0, i))
    return pl.pallas_call(
        project_kernel,
        grid=(width // tile,),
        out_shape=[
            jax.ShapeDtypeStruct((half, width), BF16),
            jax.ShapeDtypeStruct((half, width), BF16),
            jax.ShapeDtypeStruct((rows, width), F32),
        ],
        in_specs=[pl.BlockSpec((rows, width), lambda i: (0, 0)), col(width)],
        out_specs=[col(half), col(half), col(rows)],
        compiler_params=pltpu.CompilerParams(vmem_limit_bytes=VMEM_LIMIT),
        cost_estimate=cost(2 * rows * width * width, 2 * width * width),
        name="project",
    )(x, w)


def pick_rows(first_ref, ids, blocks, base, out_ref):
    picks = []
    for n, block in enumerate(blocks):
        lane = lax.broadcasted_iota(jnp.int32, (ids.shape[0], block.shape[0]), 1)
        picks.append(((ids - first_ref[n]) == lane).astype(BF16))
    width = out_ref.shape[1]
    step = chunk_of(width)
    for c in range(0, width, step):
        cols = slice(c, c + step)
        rows = sum(dot(p, block[:, cols]) for p, block in zip(picks, blocks))
        if base is not None:
            rows = rows + base[:, cols].astype(F32)
        out_ref[:, cols] = rows.astype(BF16)


def first_rows_kernel(n, first_ref, ids_ref, *refs):
    pick_rows(first_ref, ids_ref[...], refs[:n], None, refs[n])


def score_kernel(n, slots, users, scale, first_ref, ids_ref, here_ref, base_ref, *refs):
    blocks = refs[:n]
    z_slots = refs[n : n + slots]
    rows_ref, z_ref, logit_ref, pos_ref, stat_ref = refs[n + slots :]
    half = z_slots[0].shape[0]
    for k, slot in enumerate(z_slots):
        z_ref[k * half : (k + 1) * half] = slot[...]
    pick_rows(first_ref, ids_ref[...], blocks, base_ref, rows_ref)
    width = z_ref.shape[1]
    step = chunk_of(width)
    lanes = min(width, 128)
    logits = 0.0
    pos = jnp.zeros((users, lanes), F32)
    for c in range(0, width, step):
        z = z_ref[:, c : c + step]
        logits = logits + dot(rows_ref[users:, c : c + step], z, 1, 1)
        prod = z.astype(F32) * rows_ref[:users, c : c + step].astype(F32)
        for d in range(0, step, lanes):
            pos = pos + prod[:, d : d + lanes]
    logits = logits * scale
    pos = scale * jnp.sum(jnp.transpose(pos), axis=0, keepdims=True)
    here = here_ref[...] > 0
    top = jnp.max(logits, axis=0, keepdims=True)
    top = jnp.where(here, jnp.maximum(top, pos), top)
    total = jnp.sum(jnp.exp(logits - top), axis=0, keepdims=True)
    total = total + jnp.where(here, jnp.exp(pos - top), 0.0)
    logit_ref[...] = logits
    pos_ref[...] = pos
    stat_ref[0:1] = top
    stat_ref[1:2] = total


def weigh_kernel(chips, users, mine, scale, here_ref, logit_ref, pos_ref, rows_ref, *refs):
    stats = refs[:chips]
    own_ref, other_ref, weight_ref = refs[chips : chips + 3]
    parts = refs[chips + 3 :]
    half = users // (2 * chips)
    side = chips * half
    tops, totals = [], []
    for k in range(chips):
        stat = stats[k][...]
        up, down = stat[:, :side], stat[:, side:]
        cut = k * half
        if cut:
            up = jnp.concatenate([up[:, side - cut :], up[:, : side - cut]], axis=1)
            down = jnp.concatenate([down[:, cut:], down[:, :cut]], axis=1)
        stat = jnp.concatenate([up, down], axis=1)
        tops.append(stat[0:1])
        totals.append(stat[1:2])
    peak = functools.reduce(jnp.maximum, tops)
    log_total = peak + jnp.log(sum(t * jnp.exp(m - peak) for m, t in zip(tops, totals)))
    prob = jnp.exp(logit_ref[...] - log_total).astype(BF16)
    weight = jnp.where(here_ref[...] > 0, jnp.exp(pos_ref[...] - log_total) - 1.0, 0.0)
    own_ref[...] = prob[:mine]
    other_ref[...] = prob[mine:]
    weight_ref[...] = weight
    column = jnp.transpose(jnp.broadcast_to(weight, (128, users)))[:, 0:1]
    prob = jnp.transpose(prob.astype(F32)).astype(BF16)
    width = rows_ref.shape[1]
    step = chunk_of(width)
    for c in range(0, width, step):
        cols = slice(c, c + step)
        grad = dot(prob, rows_ref[users:, cols])
        grad = scale * (grad + column * rows_ref[:users, cols].astype(F32))
        for k in range(2 * chips):
            parts[k][:, cols] = grad[k * half : (k + 1) * half].astype(parts[k].dtype)


def item_kernel(scale, first_ref, neg_ref, *refs):
    sides = [refs[4 * s : 4 * s + 4] for s in range(2)]
    outs = refs[8:]
    own_rows = sum(o.shape[0] for o in outs)
    width = outs[0].shape[1]
    first = first_ref[0]
    neg = neg_ref[...] - first
    pick = lax.broadcasted_iota(jnp.int32, (own_rows, neg.shape[1]), 0) == neg
    pick = pick.astype(F32).astype(BF16)
    weights = []
    for ids_ref, prob_ref, weight_ref, _ in sides:
        ids = ids_ref[...] - first
        row = lax.broadcasted_iota(jnp.int32, (own_rows, ids.shape[1]), 0)
        w = dot(pick, prob_ref[...]) + jnp.where(row == ids, weight_ref[...], 0.0)
        weights.append(w.astype(BF16))
    step = chunk_of(width)
    for c in range(0, width, step):
        cols = slice(c, c + step)
        grad = scale * sum(dot(w, side[3][:, cols]) for w, side in zip(weights, sides))
        at = 0
        for o in outs:
            o[:, cols] = grad[at : at + o.shape[0]].astype(o.dtype)
            at += o.shape[0]


def finish_kernel(up_ref, up_in_ref, down_ref, down_in_ref, hidden_ref, w_ref, out_ref, gh_ref):
    @pl.when(pl.program_id(0) == 0)
    def _():
        half = up_ref.shape[0]
        for at, a, b in ((0, up_ref, up_in_ref), (half, down_ref, down_in_ref)):
            hidden = hidden_ref[at : at + half]
            s = jax.nn.sigmoid(hidden)
            slope = s * (1.0 + hidden * (1.0 - s))
            gh_ref[at : at + half] = ((a[...] + b[...].astype(F32)) * slope).astype(BF16)

    out_ref[...] = dot(gh_ref[...], w_ref[...], 1, 1).astype(BF16)


def finish(up, up_in, down, down_in, hidden, w):
    rows, width = hidden.shape
    tile = min(width, 256)
    whole = lambda n: pl.BlockSpec((n, width), lambda i: (0, 0))
    return pl.pallas_call(
        finish_kernel,
        grid=(width // tile,),
        out_shape=jax.ShapeDtypeStruct((rows, width), BF16),
        in_specs=[whole(rows // 2)] * 4
        + [whole(rows), pl.BlockSpec((tile, width), lambda i: (i, 0))],
        out_specs=pl.BlockSpec((rows, tile), lambda i: (0, i)),
        scratch_shapes=[pltpu.VMEM((rows, width), BF16)],
        compiler_params=pltpu.CompilerParams(vmem_limit_bytes=VMEM_LIMIT),
        cost_estimate=cost(2 * rows * width * width, 2 * width * width),
        name="finish",
    )(up, up_in, down, down_in, hidden, w)


def ring_shift(x, step, chips, name):
    perm = [
        (chip * 2 + core, (chip + step) % chips * 2 + core)
        for chip in range(chips)
        for core in range(2)
    ]
    with jax.named_scope(name):
        return lax.ppermute(x, "mem", perm)


def core_swap(x, members, name):
    with jax.named_scope(name):
        return lax.ppermute(x, "mem", [(m, m ^ 1) for m in range(members)])


def group_swap(x, bits, groups, name):
    with jax.named_scope(name):
        return lax.ppermute(x, "grp", [(g, g ^ bits) for g in range(groups)])


def low_bit(k):
    return k & -k


def on_device(user_rows, projection, item_table, positive, negatives):
    groups = lax.axis_size("grp")
    members = lax.axis_size("mem")
    chips = members // 2
    rows_here, width = user_rows.shape
    half = rows_here // 2
    users = chips * rows_here
    own_rows = item_table.shape[0]
    mid = own_rows // 2
    neg_rows = negatives.shape[1]
    scale = 4.0 / math.sqrt(width)
    g = lax.axis_index("grp")
    m = lax.axis_index("mem")
    single = [k for k in range(1, groups) if low_bit(k) == k]
    double = [k for k in range(1, groups) if low_bit(k) != k]

    block = {0: [(0, item_table)]}
    for k in single:
        block[k] = [(0, group_swap(item_table, k, groups, f"i{k}"))]
    z_up, z_down, hidden = project(user_rows, projection)
    z_ups, z_downs = [z_up], [z_down]
    for k in range(1, chips):
        z_ups.append(ring_shift(z_ups[-1], 1, chips, f"za{k}"))
        z_downs.append(ring_shift(z_downs[-1], -1, chips, f"zb{k}"))
    ids_in = [positive] + [ring_shift(positive, k, chips, f"d{k}") for k in range(1, chips)]
    ids = jnp.concatenate(
        [ids_in[k][:half] for k in range(chips)] + [ids_in[-k % chips][half:] for k in range(chips)]
    )
    neg_own = [jnp.take(negatives, g, axis=0)]
    for k in range(1, groups):
        neg_own.append(group_swap(jnp.take(negatives, g ^ k, axis=0), k, groups, f"n{k}"))
    neg_own = jnp.concatenate(neg_own)
    id_sib = core_swap(jnp.concatenate([ids, neg_own]), members, "ds")
    ids_other, neg_other = id_sib[:users], id_sib[users:]
    for k in double:
        low = low_bit(k)
        rest = k ^ low
        block[k] = [
            (0, group_swap(block[rest][0][1][:mid], low, groups, f"i{k}a")),
            (mid, group_swap(block[low][0][1][mid:], rest, groups, f"i{k}b")),
        ]

    def first_of(k, member):
        return ((g ^ k) * members + member) * own_rows

    def stage(ks):
        own = [(first_of(k, m) + at, rows) for k in ks for at, rows in block[k]]
        other = [
            (first_of(k, m ^ 1) + at, core_swap(rows, members, f"c{k}{at}"))
            for k in ks
            for at, rows in block[k]
        ]
        return jnp.stack([f for f, _ in own + other]).astype(jnp.int32), [r for _, r in own + other]

    early = [0] + single
    first_early, early_blocks = stage(early)
    first_late, late_blocks = stage(double)
    sel = jnp.concatenate([ids, neg_own, neg_other])[:, None]
    here = ((ids // (2 * own_rows)) % chips == m // 2).astype(jnp.int32)[None]
    names = sel.shape[0]
    (base,) = call(
        functools.partial(first_rows_kernel, len(early_blocks)),
        [((names, width), BF16)],
        1,
        [first_early, sel] + early_blocks,
        2 * names * width * own_rows * len(early_blocks),
        2 * width * (names + own_rows * len(early_blocks)),
        "first_rows",
    )
    negs = names - users
    rows, z_all, logits, pos, stat = call(
        functools.partial(score_kernel, len(late_blocks), 2 * chips, users, scale),
        [
            ((names, width), BF16),
            ((users, width), BF16),
            ((negs, users), F32),
            ((1, users), F32),
            ((2, users), F32),
        ],
        1,
        [first_late, sel, here, base] + late_blocks + z_ups + z_downs,
        2 * names * width * own_rows * len(late_blocks) // 2 + 2 * users * negs * width,
        2 * width * (names * 2 + users * 2),
        "score",
    )
    stats = [stat] + [ring_shift(stat, k, chips, f"s{k}") for k in range(1, chips)]
    z_other = core_swap(z_all, members, "zs")
    mine = groups * neg_rows
    out = call(
        functools.partial(weigh_kernel, chips, users, mine, scale),
        [
            ((mine, users), BF16),
            ((mine, users), BF16),
            ((1, users), F32),
        ]
        + [((half, width), F32 if k % chips == 0 else BF16) for k in range(2 * chips)],
        0,
        [here, logits, pos, rows] + stats,
        2 * users * negs * width,
        2 * width * (names + 2 * users),
        "weigh",
    )
    prob, prob_out, weight = out[:3]
    part_up, part_down = out[3 : 3 + chips], out[3 + chips :]
    prob_in = core_swap(prob_out, members, "ps")
    weight_in = core_swap(weight, members, "ws")

    def item_part(k, kinds):
        args = [
            first_of(k, m).reshape(1).astype(jnp.int32),
            neg_own[None, k * neg_rows : (k + 1) * neg_rows],
            ids[None],
            prob[k * neg_rows : (k + 1) * neg_rows],
            weight,
            z_all,
            ids_other[None],
            prob_in[k * neg_rows : (k + 1) * neg_rows],
            weight_in,
            z_other,
        ]
        return call(
            functools.partial(item_kernel, scale),
            [((n, width), t) for n, t in kinds],
            1,
            args,
            4 * own_rows * users * width,
            2 * width * (2 * users + own_rows),
            f"item{k}",
        )

    def ring_sum(parts, step, tag):
        moving = parts[1]
        for k in range(2, chips):
            moving = ring_shift(moving, step, chips, f"{tag}{k - 1}")
            moving = (parts[k].astype(F32) + moving.astype(F32)).astype(BF16)
        return ring_shift(moving, step, chips, f"{tag}{chips - 1}")

    up_in = ring_sum(part_up, 1, "ra")
    down_in = ring_sum(part_down, -1, "rb")

    sums = {}
    for k in double:
        sums[k] = item_part(k, [(mid, BF16), (mid, BF16)])
    for k in single:
        sums[k] = item_part(k, [(mid, BF16), (mid, BF16)])
    (total,) = item_part(0, [(own_rows, F32)])
    for k in double:
        low = low_bit(k)
        rest = k ^ low
        a = group_swap(sums[k][0], low, groups, f"g{k}a")
        b = group_swap(sums[k][1], rest, groups, f"g{k}b")
        sums[rest] = [(sums[rest][0].astype(F32) + a.astype(F32)).astype(BF16), sums[rest][1]]
        sums[low] = [sums[low][0], (sums[low][1].astype(F32) + b.astype(F32)).astype(BF16)]
    got = {}
    for k in single:
        got[k] = [group_swap(piece, k, groups, f"g{k}{n}") for n, piece in enumerate(sums[k])]
    item_grad = total + sum(jnp.concatenate(got[k]).astype(F32) for k in single)
    user_grad = finish(part_up[0], up_in, part_down[0], down_in, hidden, projection)
    return (user_grad, item_grad)


def solution(mesh):
    owners = ("grp", "mem")
    return jax.shard_map(
        on_device,
        mesh=mesh,
        in_specs=(P(owners, None), P(), P(owners, None), P(owners), P(None, owners)),
        out_specs=(P(owners, None), P(owners, None)),
        check_vma=False,
    )
```

```python
import functools
import math

import jax
import jax.numpy as jnp
from jax import lax
from jax.experimental import pallas as pl
from jax.experimental.pallas import tpu as pltpu
from jax.sharding import PartitionSpec as P


F32 = jnp.float32
BF16 = jnp.bfloat16
VMEM_LIMIT = 60 * 1024 * 1024
SPARE = 6 * 1024 * 1024
VM = pl.BlockSpec(memory_space=pltpu.VMEM)
SM = pl.BlockSpec(memory_space=pltpu.SMEM)


def dot(a, b, ca=1, cb=0):
    return lax.dot_general(a, b, (((ca,), (cb,)), ((), ())), preferred_element_type=F32)


def chunk_of(width):
    return width if width < 512 else 512


def cost(flops, nbytes):
    return pl.CostEstimate(flops=int(flops), bytes_accessed=int(nbytes), transcendentals=0)


def size_of(shape, dtype):
    return math.prod(shape) * jnp.dtype(dtype).itemsize


def call(kernel, outs, n_smem, args, flops):
    nbytes = sum(size_of(x.shape, x.dtype) for x in args[n_smem:])
    nbytes += sum(size_of(s, t) for s, t in outs)
    return pl.pallas_call(
        kernel,
        out_shape=[jax.ShapeDtypeStruct(s, t) for s, t in outs],
        in_specs=[SM] * n_smem + [VM] * (len(args) - n_smem),
        out_specs=[VM] * len(outs),
        compiler_params=pltpu.CompilerParams(
            vmem_limit_bytes=min(VMEM_LIMIT, nbytes * 3 // 2 + SPARE)
        ),
        cost_estimate=cost(flops, nbytes),
    )(*args)


def project_kernel(x_ref, w_ref, up_ref, down_ref, hidden_ref):
    hidden = dot(x_ref[...], w_ref[...])
    hidden_ref[...] = hidden
    z = (hidden * jax.nn.sigmoid(hidden)).astype(BF16)
    half = up_ref.shape[0]
    up_ref[...] = z[:half]
    down_ref[...] = z[half:]


def project(x, w):
    rows, width = x.shape
    half = rows // 2
    tile = min(width, 1024)
    col = lambda n: pl.BlockSpec((n, tile), lambda i: (0, i))
    return pl.pallas_call(
    project_kernel,
    grid=(width // tile,),
    out_shape=[
        jax.ShapeDtypeStruct((half, width), BF16),
        jax.ShapeDtypeStruct((half, width), BF16),
        jax.ShapeDtypeStruct((rows, width), F32),
    ],
    in_specs=[pl.BlockSpec((rows, width), lambda i: (0, 0)), col(width)],
    out_specs=[col(half), col(half), col(rows)],
    compiler_params=pltpu.CompilerParams(vmem_limit_bytes=VMEM_LIMIT // 3),
    cost_estimate=cost(2 * rows * width * width, 2 * width * width),
    name="project",
    )(x, w)


def hits(ids, first, block):
    lane = lax.broadcasted_iota(jnp.int32, (ids.shape[0], block.shape[0]), 1)
    return ((ids - first) == lane).astype(BF16)


def pick_kernel(n, based, first_ref, ids_ref, neg_ref, *refs):
    blocks = refs[:n]
    base_ref = refs[n] if based else None
    pos_ref, rows_ref = refs[n + based :]
    pick_rows(first_ref, ids_ref, neg_ref, blocks, 1, base_ref, [pos_ref], [rows_ref], [0])


def pick_rows(first_ref, ids_ref, neg_ref, blocks, run, base_ref, pos_refs, row_refs, row_at):
    ids, neg = ids_ref[...], neg_ref[...]
    picks = [hits(ids, first_ref[n], block) for n, block in enumerate(blocks)]
    owners = len(blocks) // run
    each = neg.shape[0] // owners
    neg_picks = [
        hits(neg[n // run * each : (n // run + 1) * each], first_ref[n], block)
        for n, block in enumerate(blocks)
    ]
    width = blocks[0].shape[1]
    step = chunk_of(width)
    cut = ids.shape[0] // len(pos_refs)
    for c in range(0, width, step):
        cols = slice(c, c + step)
        rows = sum(dot(p, block[:, cols]) for p, block in zip(picks, blocks))
        if base_ref is not None:
            rows = rows + base_ref[:, cols].astype(F32)
        rows = rows.astype(BF16)
        for k, pos_ref in enumerate(pos_refs):
            pos_ref[:, cols] = rows[k * cut : (k + 1) * cut]
        for o in range(owners):
            mine = range(o * run, (o + 1) * run)
            got = sum(dot(neg_picks[n], blocks[n][:, cols]) for n in mine)
            at = row_at[0] + o * each
            row_refs[0][at : at + each, cols] = got.astype(BF16)


def scores(scale, z_of, neg_ref, pos_refs, here, logit_ref, pos_out):
    width = neg_ref.shape[1]
    step = chunk_of(width)
    lanes = min(width, 128)
    slot = pos_refs[0].shape[0]
    logits = 0.0
    pos = [jnp.zeros((slot, lanes), F32) for _ in pos_refs]
    for c in range(0, width, step):
        cols = slice(c, c + step)
        z = z_of(cols)
        logits = logits + dot(neg_ref[:, cols], z, 1, 1)
        for k, ref in enumerate(pos_refs):
            prod = z[k * slot : (k + 1) * slot].astype(F32) * ref[:, cols].astype(F32)
            for d in range(0, step, lanes):
                pos[k] = pos[k] + prod[:, d : d + lanes]
    logits = logits * scale
    pos = [scale * jnp.sum(jnp.transpose(p), axis=0, keepdims=True) for p in pos]
    pos = pos[0] if len(pos) == 1 else jnp.concatenate(pos, axis=1)
    top = jnp.max(logits, axis=0, keepdims=True)
    top = jnp.where(here, jnp.maximum(top, pos), top)
    total = jnp.sum(jnp.exp(logits - top), axis=0, keepdims=True)
    total = total + jnp.where(here, jnp.exp(pos - top), 0.0)
    logit_ref[...] = logits
    pos_out[...] = pos
    return top, total


def main_kernel(n, slots, run, scale, first_ref, ids_ref, neg_ref, here_ref, base_ref, *refs):
    early = refs[:2]
    blocks = refs[2 : 2 + n]
    zs = refs[2 + n : 2 + n + 2 * slots]
    rest = refs[2 + n + 2 * slots :]
    pos_refs, (neg_out, logit_ref, pos_out, stat_ref) = rest[: slots + 1], rest[slots + 1 :]
    at = 0
    for e in early:
        neg_out[at : at + e.shape[0]] = e[...]
        at += e.shape[0]
    pick_rows(first_ref, ids_ref, neg_ref, blocks, run, base_ref, pos_refs, [neg_out], [at])

    def z_of(cols):
        return jnp.concatenate([z[:, cols] for z in zs], axis=0)

    users = slots * pos_refs[0].shape[0]
    here = here_ref[:, :users] > 0
    top, total = scores(scale, z_of, neg_out, pos_refs[:slots], here, logit_ref, pos_out)
    stat_ref[0:1] = top
    stat_ref[1:2] = total


def tail_kernel(scale, here_ref, neg_ref, pos_ref, up_ref, down_ref, stat_in, *refs):
    logit_ref, pos_out, stat_ref = refs

    def z_of(cols):
        return jnp.concatenate([up_ref[:, cols], down_ref[:, cols]], axis=0)

    slot = pos_ref.shape[0]
    users = here_ref.shape[1]
    here = here_ref[:, users - slot :] > 0
    top, total = scores(scale, z_of, neg_ref, [pos_ref], here, logit_ref, pos_out)
    stat_ref[:, : users - slot] = stat_in[...]
    stat_ref[0:1, users - slot :] = top
    stat_ref[1:2, users - slot :] = total


def join_kernel(*refs):
    out = refs[-1]
    at = 0
    for r in refs[:-1]:
        out[at : at + r.shape[0]] = r[...]
        at += r.shape[0]


def slot_total(stats, chips, k, slot):
    half = slot // 2
    tops, totals = [], []
    for s in range(chips):
        up = (k - s) % chips * slot
        down = (k + s) % chips * slot + half
        stat = jnp.concatenate(
            [stats[s][:, up : up + half], stats[s][:, down : down + half]], axis=1
        )
        tops.append(stat[0:1])
        totals.append(stat[1:2])
    peak = functools.reduce(jnp.maximum, tops)
    return peak + jnp.log(sum(t * jnp.exp(m - peak) for m, t in zip(tops, totals)))


def slot_weights(stats, chips, k, slot, logit, pos, here):
    log_total = slot_total(stats, chips, k, slot)
    prob = jnp.exp(logit - log_total).astype(BF16)
    weight = jnp.where(here > 0, jnp.exp(pos - log_total) - 1.0, 0.0)
    return prob, weight


def slot_grad(scale, prob, weight, neg_ref, pos_ref, up_ref, down_ref):
    slot, width = pos_ref.shape
    half = slot // 2
    column = jnp.transpose(jnp.broadcast_to(weight, (128, slot)))[:, 0:1]
    prob = jnp.transpose(prob.astype(F32)).astype(BF16)
    step = chunk_of(width)
    for c in range(0, width, step):
        cols = slice(c, c + step)
        grad = dot(prob, neg_ref[:, cols]) + column * pos_ref[:, cols].astype(F32)
        grad = scale * grad
        up_ref[:, cols] = grad[:half].astype(up_ref.dtype)
        down_ref[:, cols] = grad[half:].astype(down_ref.dtype)


def lead_kernel(chips, scale, here_ref, logit_ref, pos_ref, neg_ref, rows_ref, *refs):
    stats, (up_ref, down_ref) = refs[:chips], refs[chips:]
    slot = rows_ref.shape[0]
    lanes = slice(slot, 2 * slot)
    prob, weight = slot_weights(
        stats, chips, 1, slot, logit_ref[:, lanes], pos_ref[:, lanes], here_ref[:, lanes]
    )
    slot_grad(scale, prob, weight, neg_ref, rows_ref, up_ref, down_ref)


def rest_kernel(chips, scale, order, each, here_ref, logit_ref, pos_ref, logit_t, pos_t, *refs):
    neg_ref, refs = refs[0], refs[1:]
    rows, refs = refs[: chips - 1], refs[chips - 1 :]
    stats, refs = refs[:chips], refs[chips:]
    own_ref, other_ref, weight_ref = refs[:3]
    parts = refs[3:]
    slot = rows[0].shape[0]
    at = 0
    for k in range(chips):
        lanes = slice(k * slot, (k + 1) * slot)
        last = k == chips - 1
        logit = logit_t[...] if last else logit_ref[:, lanes]
        pos = pos_t[...] if last else pos_ref[:, lanes]
        prob, weight = slot_weights(stats, chips, k, slot, logit, pos, here_ref[:, lanes])
        weight_ref[:, lanes] = weight
        for n, (side, owner) in enumerate(order):
            to = other_ref if side else own_ref
            to[owner * each : (owner + 1) * each, lanes] = prob[n * each : (n + 1) * each]
        if k != 1:
            slot_grad(scale, prob, weight, neg_ref, rows[at], parts[2 * at], parts[2 * at + 1])
            at += 1


def item_kernel(scale, first_ref, neg_ref, *refs):
    sides = [refs[4 * s : 4 * s + 4] for s in range(2)]
    outs = refs[8:]
    own_rows = sum(o.shape[0] for o in outs)
    width = outs[0].shape[1]
    first = first_ref[0]
    neg = neg_ref[...] - first
    pick = lax.broadcasted_iota(jnp.int32, (own_rows, neg.shape[1]), 0) == neg
    pick = pick.astype(F32).astype(BF16)
    weights = []
    for ids_ref, prob_ref, weight_ref, _ in sides:
        ids = ids_ref[...] - first
        row = lax.broadcasted_iota(jnp.int32, (own_rows, ids.shape[1]), 0)
        w = dot(pick, prob_ref[...]) + jnp.where(row == ids, weight_ref[...], 0.0)
        weights.append(w.astype(BF16))
    step = chunk_of(width)
    for c in range(0, width, step):
        cols = slice(c, c + step)
        grad = scale * sum(dot(w, side[3][:, cols]) for w, side in zip(weights, sides))
        at = 0
        for o in outs:
            o[:, cols] = grad[at : at + o.shape[0]].astype(o.dtype)
            at += o.shape[0]


def finish_kernel(up_ref, up_in_ref, down_ref, down_in_ref, hidden_ref, w_ref, out_ref, gh_ref):
    @pl.when(pl.program_id(0) == 0)
    def _():
        half = up_ref.shape[0]
        for at, a, b in ((0, up_ref, up_in_ref), (half, down_ref, down_in_ref)):
            hidden = hidden_ref[at : at + half]
            s = jax.nn.sigmoid(hidden)
            slope = s * (1.0 + hidden * (1.0 - s))
            gh_ref[at : at + half] = ((a[...] + b[...].astype(F32)) * slope).astype(BF16)

    out_ref[...] = dot(gh_ref[...], w_ref[...], 1, 1).astype(BF16)


def finish(up, up_in, down, down_in, hidden, w):
    rows, width = hidden.shape
    tile = min(width, 1024)
    whole = lambda n: pl.BlockSpec((n, width), lambda i: (0, 0))
    return pl.pallas_call(
        finish_kernel,
        grid=(width // tile,),
        out_shape=jax.ShapeDtypeStruct((rows, width), BF16),
        in_specs=[whole(rows // 2)] * 4
        + [whole(rows), pl.BlockSpec((tile, width), lambda i: (i, 0))],
        out_specs=pl.BlockSpec((rows, tile), lambda i: (0, i)),
        scratch_shapes=[pltpu.VMEM((rows, width), BF16)],
        compiler_params=pltpu.CompilerParams(vmem_limit_bytes=VMEM_LIMIT // 3),
        cost_estimate=cost(2 * rows * width * width, 2 * width * width),
        name="finish",
    )(up, up_in, down, down_in, hidden, w)


def ring_shift(x, step, chips):
    perm = [
        (chip * 2 + core, (chip + step) % chips * 2 + core)
        for chip in range(chips)
        for core in range(2)
    ]
    return lax.ppermute(x, "mem", perm)


def core_swap(x, members):
    return lax.ppermute(x, "mem", [(m, m ^ 1) for m in range(members)])


def group_swap(x, bits, groups):
    return lax.ppermute(x, "grp", [(g, g ^ bits) for g in range(groups)])


def low_bit(k):
    return k & -k


def on_device(user_rows, projection, item_table, positive, negatives):
    groups = lax.axis_size("grp")
    members = lax.axis_size("mem")
    chips = members // 2
    rows_here, width = user_rows.shape
    half = rows_here // 2
    users = chips * rows_here
    own_rows = item_table.shape[0]
    mid = own_rows // 2
    neg_rows = negatives.shape[1]
    scale = 4.0 / math.sqrt(width)
    g = lax.axis_index("grp")
    m = lax.axis_index("mem")
    single = [k for k in range(1, groups) if low_bit(k) == k]
    double = [k for k in range(1, groups) if low_bit(k) != k]

    block = {0: [(0, item_table)]}
    for k in single:
        block[k] = [(0, group_swap(item_table, k, groups))]
    z_up, z_down, hidden = project(user_rows, projection)
    z_ups, z_downs = [z_up], [z_down]
    for _ in range(1, chips):
        z_ups.append(ring_shift(z_ups[-1], 1, chips))
        z_downs.append(ring_shift(z_downs[-1], -1, chips))
    z_slots = [z for pair in zip(z_ups, z_downs) for z in pair]
    ids_in = [positive] + [ring_shift(positive, k, chips) for k in range(1, chips)]
    ids = jnp.concatenate(
        [x for k in range(chips) for x in (ids_in[k][:half], ids_in[-k % chips][half:])]
    )
    neg_own = [jnp.take(negatives, g, axis=0)]
    for k in range(1, groups):
        neg_own.append(group_swap(jnp.take(negatives, g ^ k, axis=0), k, groups))
    id_sib = core_swap(jnp.concatenate([ids] + neg_own), members)
    ids_other = id_sib[:users]
    neg_other = [id_sib[users + k * neg_rows : users + (k + 1) * neg_rows] for k in range(groups)]
    for k in double:
        low = low_bit(k)
        rest = k ^ low
        block[k] = [
            (0, group_swap(block[rest][0][1][:mid], low, groups)),
            (mid, group_swap(block[low][0][1][mid:], rest, groups)),
        ]

    def first_of(k, member):
        return ((g ^ k) * members + member) * own_rows

    order = []

    def stage(ks):
        firsts, rows, negs = [], [], []
        for side in range(2):
            for k in ks:
                order.append((side, k))
                negs.append(neg_other[k] if side else neg_own[k])
                for at, piece in block[k]:
                    firsts.append(first_of(k, m ^ 1 if side else m) + at)
                    rows.append(core_swap(piece, members) if side else piece)
        return jnp.stack(firsts).astype(jnp.int32), jnp.concatenate(negs)[:, None], rows

    sel = ids[:, None]
    here = ((ids // (2 * own_rows)) % chips == m // 2).astype(jnp.int32)[None]
    slots = chips - 1
    base, early = None, []
    for ks in ([0], single):
        firsts, neg_ids, rows = stage(ks)
        base, got_rows = call(
            functools.partial(pick_kernel, len(rows), int(base is not None)),
            [((users, width), BF16), ((neg_ids.shape[0], width), BF16)],
            1,
            [firsts, sel, neg_ids] + rows + ([] if base is None else [base]),
            2 * users * width * own_rows * len(rows),
        )
        early.append(got_rows)
    firsts, neg_ids, rows = stage(double)
    negs = 2 * groups * neg_rows
    out = call(
        functools.partial(main_kernel, len(rows), slots, 2, scale),
        [((rows_here, width), BF16)] * chips
        + [
            ((negs, width), BF16),
            ((negs, slots * rows_here), F32),
            ((1, slots * rows_here), F32),
            ((2, slots * rows_here), F32),
        ],
        1,
        [firsts, sel, neg_ids, here, base] + early + rows + z_slots[: 2 * slots],
        2 * users * width * mid * len(rows) + 2 * users * negs * width,
    )
    pos_rows, (neg_all, logits, pos, stat) = out[:chips], out[chips:]
    logits_t, pos_t, stat = call(
        functools.partial(tail_kernel, scale),
        [((negs, rows_here), F32), ((1, rows_here), F32), ((2, users), F32)],
        0,
        [here, neg_all, pos_rows[-1]] + z_slots[2 * slots :] + [stat],
        2 * rows_here * negs * width,
    )
    stats = [stat] + [ring_shift(stat, k, chips) for k in range(1, chips)]
    (z_all,) = call(join_kernel, [((users, width), BF16)], 0, z_slots, users * width)
    z_other = core_swap(z_all, members)
    mine = groups * neg_rows
    part = [None] * chips
    part[1] = call(
        functools.partial(lead_kernel, chips, scale),
        [((half, width), BF16)] * 2,
        0,
        [here, logits, pos, neg_all, pos_rows[1]] + stats,
        2 * rows_here * negs * width,
    )
    others = [k for k in range(chips) if k != 1]
    out = call(
        functools.partial(rest_kernel, chips, scale, tuple(order), neg_rows),
        [((mine, users), BF16), ((mine, users), BF16), ((1, users), F32)]
        + [((half, width), BF16 if k else F32) for k in others for _ in range(2)],
        0,
        [here, logits, pos, logits_t, pos_t, neg_all] + [pos_rows[k] for k in others] + stats,
        2 * users * negs * width,
    )
    prob, prob_out, weight = out[:3]
    for n, k in enumerate(others):
        part[k] = out[3 + 2 * n : 5 + 2 * n]
    prob_in = core_swap(prob_out, members)
    weight_in = core_swap(weight, members)

    def item_part(k, kinds):
        args = [
            first_of(k, m).reshape(1).astype(jnp.int32),
            neg_own[k][None],
            ids[None],
            prob[k * neg_rows : (k + 1) * neg_rows],
            weight,
            z_all,
            ids_other[None],
            prob_in[k * neg_rows : (k + 1) * neg_rows],
            weight_in,
            z_other,
        ]
        return call(
            functools.partial(item_kernel, scale),
            [((n, width), t) for n, t in kinds],
            1,
            args,
            4 * own_rows * users * width,
        )

    def ring_sum(side, step):
        moving = part[1][side]
        for k in range(2, chips):
            moving = ring_shift(moving, step, chips)
            moving = (part[k][side].astype(F32) + moving.astype(F32)).astype(BF16)
        return ring_shift(moving, step, chips)

    up_in = ring_sum(0, 1)
    down_in = ring_sum(1, -1)

    sums = {}
    for k in double + single:
        sums[k] = item_part(k, [(mid, BF16), (mid, BF16)])
    (total,) = item_part(0, [(own_rows, F32)])
    for k in double:
        low = low_bit(k)
        rest = k ^ low
        a = group_swap(sums[k][0], low, groups)
        b = group_swap(sums[k][1], rest, groups)
        sums[rest] = [(sums[rest][0].astype(F32) + a.astype(F32)).astype(BF16), sums[rest][1]]
        sums[low] = [sums[low][0], (sums[low][1].astype(F32) + b.astype(F32)).astype(BF16)]
    got = {}
    for k in single:
        got[k] = [group_swap(piece, k, groups) for piece in sums[k]]
    item_grad = total + sum(jnp.concatenate(got[k]).astype(F32) for k in single)
    user_grad = finish(part[0][0], up_in, part[0][1], down_in, hidden, projection)
    return (user_grad, item_grad)


def solution(mesh):
    owners = ("grp", "mem")

    return jax.shard_map(
        on_device,
        mesh=mesh,
        in_specs=(P(owners, None), P(), P(owners, None), P(owners), P(None, owners)),
        out_specs=(P(owners, None), P(owners, None)),
        check_vma=False,
    )
```

```python
import functools
import math

import jax
import jax.numpy as jnp
from jax import lax
from jax.experimental import pallas as pl
from jax.experimental.pallas import tpu as pltpu
from jax.sharding import PartitionSpec as P


F32 = jnp.float32
BF16 = jnp.bfloat16
VMEM_LIMIT = 60 * 1024 * 1024
SPARE = 6 * 1024 * 1024
VM = pl.BlockSpec(memory_space=pltpu.VMEM)
SM = pl.BlockSpec(memory_space=pltpu.SMEM)


def dot(a, b, ca=1, cb=0):
    return lax.dot_general(a, b, (((ca,), (cb,)), ((), ())), preferred_element_type=F32)


def chunk_of(width):
    return width if width < 512 else 512


def cost(flops, nbytes):
    return pl.CostEstimate(flops=int(flops), bytes_accessed=int(nbytes), transcendentals=0)


def size_of(shape, dtype):
    return math.prod(shape) * jnp.dtype(dtype).itemsize


def call(kernel, outs, n_smem, args, flops):
    nbytes = sum(size_of(x.shape, x.dtype) for x in args[n_smem:])
    nbytes += sum(size_of(s, t) for s, t in outs)
    return pl.pallas_call(
        kernel,
        out_shape=[jax.ShapeDtypeStruct(s, t) for s, t in outs],
        in_specs=[SM] * n_smem + [VM] * (len(args) - n_smem),
        out_specs=[VM] * len(outs),
        compiler_params=pltpu.CompilerParams(
            vmem_limit_bytes=min(VMEM_LIMIT, nbytes * 3 // 2 + SPARE)
        ),
        cost_estimate=cost(flops, nbytes),
    )(*args)


def project_kernel(x_up, x_down, w_ref, z_ref, *hidden_ref):
    x = jnp.concatenate([x_up[...], x_down[...]], axis=0)
    width = w_ref.shape[1]
    step = chunk_of(width)
    for c in range(0, width, step):
        cols = slice(c, c + step)
        hidden = dot(x, w_ref[:, cols])
        if hidden_ref:
            hidden_ref[0][:, cols] = hidden
        z_ref[:, cols] = (hidden * jax.nn.sigmoid(hidden)).astype(BF16)


def first_of(k, side, own_rows):
    g, m = lax.axis_index("grp"), lax.axis_index("mem")
    return ((g ^ k) * lax.axis_size("mem") + (m ^ side)) * own_rows


def column(row):
    tall = jnp.broadcast_to(row.astype(F32), (128, row.shape[1]))
    return jnp.transpose(tall)[:, 0:1].astype(jnp.int32)


def ids_kernel(chips, *refs):
    pos, neg, out = refs[:chips], refs[chips:-1], refs[-1]
    half = pos[0].shape[1] // 2
    row = []
    for k in range(chips):
        row += [pos[k][:, :half], pos[-k % chips][:, half:]]
    out[0:1] = jnp.concatenate(row, axis=1)
    g = lax.axis_index("grp")
    row = jnp.concatenate([n[pl.ds(g, 1)] for n in neg], axis=1)
    out[1:2, : row.shape[1]] = row


def is_here(ids, own_rows):
    here = None
    for k in range(lax.axis_size("grp")):
        low = jnp.minimum(first_of(k, 0, own_rows), first_of(k, 1, own_rows))
        hit = (ids >= low) & (ids < low + 2 * own_rows)
        here = hit if here is None else here | hit
    return here


def hits(ids, first, block):
    lane = lax.broadcasted_iota(jnp.int32, (ids.shape[0], block.shape[0]), 1)
    return ((ids - first) == lane).astype(BF16)


def pick_kernel(plan, own_rows, each, own_ref, other_ref, *refs):
    n = len(plan)
    blocks = refs[:n]
    base_ref = refs[n] if len(refs) > n + 2 else None
    pick_rows(plan, own_rows, each, own_ref, other_ref, blocks, base_ref, [refs[-2]], refs[-1], 0)


def pick_rows(plan, own_rows, each, own_ref, other_ref, blocks, base_ref, pos_refs, row_ref, at):
    users = own_ref.shape[1]
    ids = column(own_ref[0:1])
    many = each * lax.axis_size("grp")
    neg = [column(r[1:2, :many]) for r in (own_ref, other_ref)]
    firsts = [first_of(k, side, own_rows) + row for side, k, row in plan]
    picks = [hits(ids, f, block) for f, block in zip(firsts, blocks)]
    owners = list(dict.fromkeys((side, k) for side, k, _ in plan))
    neg_picks = [
        hits(neg[side][k * each : (k + 1) * each], f, block)
        for (side, k, _), f, block in zip(plan, firsts, blocks)
    ]
    width = blocks[0].shape[1]
    step = chunk_of(width)
    cut = users // len(pos_refs)
    for c in range(0, width, step):
        cols = slice(c, c + step)
        rows = sum(dot(p, block[:, cols]) for p, block in zip(picks, blocks))
        if base_ref is not None:
            rows = rows + base_ref[:, cols].astype(F32)
        rows = rows.astype(BF16)
        for k, pos_ref in enumerate(pos_refs):
            pos_ref[:, cols] = rows[k * cut : (k + 1) * cut]
        for o, owner in enumerate(owners):
            mine = [n for n, (side, k, _) in enumerate(plan) if (side, k) == owner]
            got = sum(dot(neg_picks[n], blocks[n][:, cols]) for n in mine)
            row_ref[at + o * each : at + (o + 1) * each, cols] = got.astype(BF16)


def scores(scale, z_of, neg_ref, pos_refs, here, logit_ref, pos_out):
    width = neg_ref.shape[1]
    step = chunk_of(width)
    lanes = min(width, 128)
    slot = pos_refs[0].shape[0]
    logits = 0.0
    pos = [jnp.zeros((slot, lanes), F32) for _ in pos_refs]
    for c in range(0, width, step):
        cols = slice(c, c + step)
        z = z_of(cols)
        logits = logits + dot(neg_ref[:, cols], z, 1, 1)
        for k, ref in enumerate(pos_refs):
            prod = z[k * slot : (k + 1) * slot].astype(F32) * ref[:, cols].astype(F32)
            for d in range(0, step, lanes):
                pos[k] = pos[k] + prod[:, d : d + lanes]
    logits = logits * scale
    pos = [scale * jnp.sum(jnp.transpose(p), axis=0, keepdims=True) for p in pos]
    pos = pos[0] if len(pos) == 1 else jnp.concatenate(pos, axis=1)
    top = jnp.max(logits, axis=0, keepdims=True)
    top = jnp.where(here, jnp.maximum(top, pos), top)
    total = jnp.sum(jnp.exp(logits - top), axis=0, keepdims=True)
    total = total + jnp.where(here, jnp.exp(pos - top), 0.0)
    logit_ref[...] = logits
    pos_out[...] = pos
    return top, total


def main_kernel(plan, own_rows, each, slots, scale, own_ref, other_ref, base_ref, *refs):
    n = len(plan)
    early = refs[:2]
    blocks = refs[2 : 2 + n]
    zs = refs[2 + n : 2 + n + slots]
    rest = refs[2 + n + slots :]
    pos_refs, (neg_out, logit_ref, pos_out, stat_ref) = rest[: slots + 1], rest[slots + 1 :]
    at = 0
    for e in early:
        neg_out[at : at + e.shape[0]] = e[...]
        at += e.shape[0]
    pick_rows(plan, own_rows, each, own_ref, other_ref, blocks, base_ref, pos_refs, neg_out, at)

    def z_of(cols):
        return jnp.concatenate([z[:, cols] for z in zs], axis=0)

    users = slots * pos_refs[0].shape[0]
    here = is_here(own_ref[0:1, :users], own_rows)
    top, total = scores(scale, z_of, neg_out, pos_refs[:slots], here, logit_ref, pos_out)
    stat_ref[0:1] = top
    stat_ref[1:2] = total


def tail_kernel(own_rows, scale, own_ref, neg_ref, pos_ref, z_ref, stat_in, *refs):
    logit_ref, pos_out, stat_ref = refs

    def z_of(cols):
        return z_ref[:, cols]

    slot = pos_ref.shape[0]
    users = own_ref.shape[1]
    here = is_here(own_ref[0:1, users - slot :], own_rows)
    top, total = scores(scale, z_of, neg_ref, [pos_ref], here, logit_ref, pos_out)
    stat_ref[:, : users - slot] = stat_in[...]
    stat_ref[0:1, users - slot :] = top
    stat_ref[1:2, users - slot :] = total


def join_kernel(*refs):
    out = refs[-1]
    at = 0
    for r in refs[:-1]:
        out[at : at + r.shape[0]] = r[...]
        at += r.shape[0]


def slot_total(stats, chips, k, slot):
    half = slot // 2
    tops, totals = [], []
    for s in range(chips):
        up = (k - s) % chips * slot
        down = (k + s) % chips * slot + half
        stat = jnp.concatenate(
            [stats[s][:, up : up + half], stats[s][:, down : down + half]], axis=1
        )
        tops.append(stat[0:1])
        totals.append(stat[1:2])
    peak = functools.reduce(jnp.maximum, tops)
    return peak + jnp.log(sum(t * jnp.exp(m - peak) for m, t in zip(tops, totals)))


def slot_weights(stats, chips, k, slot, logit, pos, here):
    log_total = slot_total(stats, chips, k, slot)
    prob = jnp.exp(logit - log_total).astype(BF16)
    weight = jnp.where(here, jnp.exp(pos - log_total) - 1.0, 0.0)
    return prob, weight


def slot_grad(scale, prob, weight, neg_ref, pos_ref, up_ref, down_ref):
    slot, width = pos_ref.shape
    half = slot // 2
    tall = jnp.transpose(jnp.broadcast_to(weight, (128, slot)))[:, 0:1]
    prob = jnp.transpose(prob.astype(F32)).astype(BF16)
    step = chunk_of(width)
    for c in range(0, width, step):
        cols = slice(c, c + step)
        grad = dot(prob, neg_ref[:, cols]) + tall * pos_ref[:, cols].astype(F32)
        grad = scale * grad
        up_ref[:, cols] = grad[:half].astype(up_ref.dtype)
        down_ref[:, cols] = grad[half:].astype(down_ref.dtype)


def lead_kernel(chips, own_rows, scale, own_ref, logit_ref, pos_ref, neg_ref, rows_ref, *refs):
    stats, (up_ref, down_ref) = refs[:chips], refs[chips:]
    slot = rows_ref.shape[0]
    lanes = slice(slot, 2 * slot)
    here = is_here(own_ref[0:1, lanes], own_rows)
    prob, weight = slot_weights(
        stats, chips, 1, slot, logit_ref[:, lanes], pos_ref[:, lanes], here
    )
    slot_grad(scale, prob, weight, neg_ref, rows_ref, up_ref, down_ref)


def rest_kernel(chips, own_rows, scale, order, each, own_in, logit_ref, pos_ref, logit_t, pos_t, *refs):
    neg_ref, refs = refs[0], refs[1:]
    rows, refs = refs[: chips - 1], refs[chips - 1 :]
    stats, refs = refs[:chips], refs[chips:]
    own_ref, other_ref, weight_ref = refs[:3]
    parts = refs[3:]
    slot = rows[0].shape[0]
    at = 0
    for k in range(chips):
        lanes = slice(k * slot, (k + 1) * slot)
        last = k == chips - 1
        logit = logit_t[...] if last else logit_ref[:, lanes]
        pos = pos_t[...] if last else pos_ref[:, lanes]
        here = is_here(own_in[0:1, lanes], own_rows)
        prob, weight = slot_weights(stats, chips, k, slot, logit, pos, here)
        weight_ref[:, lanes] = weight
        for n, (side, owner) in enumerate(order):
            to = other_ref if side else own_ref
            to[owner * each : (owner + 1) * each, lanes] = prob[n * each : (n + 1) * each]
        if k != 1:
            slot_grad(scale, prob, weight, neg_ref, rows[at], parts[2 * at], parts[2 * at + 1])
            at += 1


def item_kernel(scale, k, each, *refs):
    sides = [refs[4 * s : 4 * s + 4] for s in range(2)]
    outs = refs[8:]
    own_rows = sum(o.shape[0] for o in outs)
    width = outs[0].shape[1]
    first = first_of(k, 0, own_rows)
    owner = slice(k * each, (k + 1) * each)
    neg = sides[0][0][1:2, owner] - first
    pick = lax.broadcasted_iota(jnp.int32, (own_rows, each), 0) == neg
    pick = pick.astype(F32).astype(BF16)
    weights = []
    for ids_ref, prob_ref, weight_ref, _ in sides:
        ids = ids_ref[0:1] - first
        row = lax.broadcasted_iota(jnp.int32, (own_rows, ids.shape[1]), 0)
        w = dot(pick, prob_ref[owner]) + jnp.where(row == ids, weight_ref[...], 0.0)
        weights.append(w.astype(BF16))
    step = chunk_of(width)
    for c in range(0, width, step):
        cols = slice(c, c + step)
        grad = scale * sum(dot(w, side[3][:, cols]) for w, side in zip(weights, sides))
        at = 0
        for o in outs:
            o[:, cols] = grad[at : at + o.shape[0]].astype(o.dtype)
            at += o.shape[0]


def finish_kernel(up_ref, up_in_ref, down_ref, down_in_ref, hidden_ref, w_ref, out_ref):
    grad = [a[...] + b[...].astype(F32) for a, b in ((up_ref, up_in_ref), (down_ref, down_in_ref))]
    hidden = hidden_ref[...]
    s = jax.nn.sigmoid(hidden)
    slope = s * (1.0 + hidden * (1.0 - s))
    grad = (jnp.concatenate(grad, axis=0) * slope).astype(BF16)
    step = chunk_of(w_ref.shape[0])
    for c in range(0, w_ref.shape[0], step):
        cols = slice(c, c + step)
        out_ref[:, cols] = dot(grad, w_ref[cols], 1, 1).astype(BF16)


def ring_shift(x, step, chips):
    perm = [
        (chip * 2 + core, (chip + step) % chips * 2 + core)
        for chip in range(chips)
        for core in range(2)
    ]
    return lax.ppermute(x, "mem", perm)


def core_swap(x, members):
    return lax.ppermute(x, "mem", [(m, m ^ 1) for m in range(members)])


def group_swap(x, bits, groups):
    return lax.ppermute(x, "grp", [(g, g ^ bits) for g in range(groups)])


def low_bit(k):
    return k & -k


def on_device(user_rows, projection, item_table, positive, negatives):
    groups = lax.axis_size("grp")
    members = lax.axis_size("mem")
    chips = members // 2
    rows_here, width = user_rows.shape
    half = rows_here // 2
    users = chips * rows_here
    own_rows = item_table.shape[0]
    mid = own_rows // 2
    neg_rows = negatives.shape[1]
    scale = 4.0 / math.sqrt(width)
    single = [k for k in range(1, groups) if low_bit(k) == k]
    double = [k for k in range(1, groups) if low_bit(k) != k]

    block = {0: [(0, item_table)]}
    for k in single:
        block[k] = [(0, group_swap(item_table, k, groups))]
    x_up, x_down = user_rows[:half], user_rows[half:]
    z_slots = []
    for k in range(chips):
        if k:
            x_up = ring_shift(x_up, 1, chips)
            x_down = ring_shift(x_down, -1, chips)
        got = call(
            project_kernel,
            [((rows_here, width), BF16)] + ([] if k else [((rows_here, width), F32)]),
            0,
            [x_up, x_down, projection],
            2 * rows_here * width * width,
        )
        z_slots.append(got[0])
        if not k:
            hidden = got[1]
    row = positive[None]
    ids_in = [row] + [ring_shift(row, k, chips) for k in range(1, chips)]
    neg_in = [negatives] + [group_swap(negatives, k, groups) for k in range(1, groups)]
    (own,) = call(
        functools.partial(ids_kernel, chips), [((2, users), jnp.int32)], 0, ids_in + neg_in, users
    )
    other = core_swap(own, members)
    for k in double:
        low = low_bit(k)
        rest = k ^ low
        block[k] = [
            (0, group_swap(block[rest][0][1][:mid], low, groups)),
            (mid, group_swap(block[low][0][1][mid:], rest, groups)),
        ]

    def stage(ks):
        plan, rows = [], []
        for side in range(2):
            for k in ks:
                for at, piece in block[k]:
                    plan.append((side, k, at))
                    rows.append(core_swap(piece, members) if side else piece)
        return tuple(plan), rows

    order = []
    slots = chips - 1
    base, early = [], []
    for ks in ([0], single):
        plan, rows = stage(ks)
        order += [(side, k) for side, k, _ in plan]
        pos_base, got_rows = call(
            functools.partial(pick_kernel, plan, own_rows, neg_rows),
            [((users, width), BF16), ((len(plan) * neg_rows, width), BF16)],
            0,
            [own, other] + rows + base,
            2 * users * width * own_rows * len(rows),
        )
        base = [pos_base]
        early.append(got_rows)
    plan, rows = stage(double)
    order += list(dict.fromkeys((side, k) for side, k, _ in plan))
    negs = 2 * groups * neg_rows
    out = call(
        functools.partial(main_kernel, plan, own_rows, neg_rows, slots, scale),
        [((rows_here, width), BF16)] * chips
        + [
            ((negs, width), BF16),
            ((negs, slots * rows_here), F32),
            ((1, slots * rows_here), F32),
            ((2, slots * rows_here), F32),
        ],
        0,
        [own, other] + base + early + rows + z_slots[:slots],
        2 * users * width * mid * len(rows) + 2 * users * negs * width,
    )
    pos_rows, (neg_all, logits, pos, stat) = out[:chips], out[chips:]
    logits_t, pos_t, stat = call(
        functools.partial(tail_kernel, own_rows, scale),
        [((negs, rows_here), F32), ((1, rows_here), F32), ((2, users), F32)],
        0,
        [own, neg_all, pos_rows[-1], z_slots[-1], stat],
        2 * rows_here * negs * width,
    )
    stats = [stat] + [ring_shift(stat, k, chips) for k in range(1, chips)]
    (z_all,) = call(join_kernel, [((users, width), BF16)], 0, z_slots, users * width)
    z_other = core_swap(z_all, members)
    mine = groups * neg_rows
    part = [None] * chips
    part[1] = call(
        functools.partial(lead_kernel, chips, own_rows, scale),
        [((half, width), BF16)] * 2,
        0,
        [own, logits, pos, neg_all, pos_rows[1]] + stats,
        2 * rows_here * negs * width,
    )
    others = [k for k in range(chips) if k != 1]
    out = call(
        functools.partial(rest_kernel, chips, own_rows, scale, tuple(order), neg_rows),
        [((mine, users), BF16), ((mine, users), BF16), ((1, users), F32)]
        + [((half, width), BF16 if k else F32) for k in others for _ in range(2)],
        0,
        [own, logits, pos, logits_t, pos_t, neg_all] + [pos_rows[k] for k in others] + stats,
        2 * users * negs * width,
    )
    prob, prob_out, weight = out[:3]
    for n, k in enumerate(others):
        part[k] = out[3 + 2 * n : 5 + 2 * n]
    prob_in = core_swap(prob_out, members)
    weight_in = core_swap(weight, members)

    def item_part(k, kinds):
        return call(
            functools.partial(item_kernel, scale, k, neg_rows),
            [((n, width), t) for n, t in kinds],
            0,
            [own, prob, weight, z_all, other, prob_in, weight_in, z_other],
            4 * own_rows * users * width,
        )

    def ring_sum(side, step):
        moving = part[1][side]
        for k in range(2, chips):
            moving = ring_shift(moving, step, chips)
            moving = (part[k][side].astype(F32) + moving.astype(F32)).astype(BF16)
        return ring_shift(moving, step, chips)

    up_in = ring_sum(0, 1)
    down_in = ring_sum(1, -1)

    sums = {}
    for k in double + single:
        sums[k] = item_part(k, [(mid, BF16), (mid, BF16)])
    (total,) = item_part(0, [(own_rows, F32)])
    for k in double:
        low = low_bit(k)
        rest = k ^ low
        a = group_swap(sums[k][0], low, groups)
        b = group_swap(sums[k][1], rest, groups)
        sums[rest] = [(sums[rest][0].astype(F32) + a.astype(F32)).astype(BF16), sums[rest][1]]
        sums[low] = [sums[low][0], (sums[low][1].astype(F32) + b.astype(F32)).astype(BF16)]
    got = {}
    for k in single:
        got[k] = [group_swap(piece, k, groups) for piece in sums[k]]
    item_grad = total + sum(jnp.concatenate(got[k]).astype(F32) for k in single)
    (user_grad,) = call(
        finish_kernel,
        [((rows_here, width), BF16)],
        0,
        [part[0][0], up_in, part[0][1], down_in, hidden, projection],
        2 * rows_here * width * width,
    )
    return (user_grad, item_grad)


def solution(mesh):
    owners = ("grp", "mem")

    return jax.shard_map(
        on_device,
        mesh=mesh,
        in_specs=(P(owners, None), P(), P(owners, None), P(owners), P(None, owners)),
        out_specs=(P(owners, None), P(owners, None)),
        check_vma=False,
    )
```

```python
import functools
import math

import jax
import jax.numpy as jnp
from jax import lax
from jax.experimental import pallas as pl
from jax.experimental.pallas import tpu as pltpu
from jax.sharding import PartitionSpec as P


F32 = jnp.float32
BF16 = jnp.bfloat16
VMEM_LIMIT = 60 * 1024 * 1024
SPARE = 6 * 1024 * 1024
VM = pl.BlockSpec(memory_space=pltpu.VMEM)
SM = pl.BlockSpec(memory_space=pltpu.SMEM)


def dot(a, b, ca=1, cb=0):
    return lax.dot_general(a, b, (((ca,), (cb,)), ((), ())), preferred_element_type=F32)


def chunk_of(width):
    return width if width < 512 else 512


def cost(flops, nbytes):
    return pl.CostEstimate(flops=int(flops), bytes_accessed=int(nbytes), transcendentals=0)


def size_of(shape, dtype):
    return math.prod(shape) * jnp.dtype(dtype).itemsize


def call(kernel, outs, n_smem, args, flops):
    nbytes = sum(size_of(x.shape, x.dtype) for x in args[n_smem:])
    nbytes += sum(size_of(s, t) for s, t in outs)
    return pl.pallas_call(
        kernel,
        out_shape=[jax.ShapeDtypeStruct(s, t) for s, t in outs],
        in_specs=[SM] * n_smem + [VM] * (len(args) - n_smem),
        out_specs=[VM] * len(outs),
        compiler_params=pltpu.CompilerParams(
            vmem_limit_bytes=min(VMEM_LIMIT, nbytes * 3 // 2 + SPARE)
        ),
        cost_estimate=cost(flops, nbytes),
    )(*args)


def project_kernel(x_up, x_down, w_ref, z_ref, *hidden_ref):
    x = jnp.concatenate([x_up[...], x_down[...]], axis=0)
    width = w_ref.shape[1]
    step = chunk_of(width)
    for c in range(0, width, step):
        cols = slice(c, c + step)
        hidden = dot(x, w_ref[:, cols])
        if hidden_ref:
            hidden_ref[0][:, cols] = hidden
        z_ref[:, cols] = (hidden * jax.nn.sigmoid(hidden)).astype(BF16)


def first_of(k, side, own_rows):
    g, m = lax.axis_index("grp"), lax.axis_index("mem")
    return ((g ^ k) * lax.axis_size("mem") + (m ^ side)) * own_rows


def column(row):
    tall = jnp.broadcast_to(row.astype(F32), (128, row.shape[1]))
    return jnp.transpose(tall)[:, 0:1].astype(jnp.int32)


def ids_kernel(chips, *refs):
    pos, neg, out = refs[:chips], refs[chips:-1], refs[-1]
    half = pos[0].shape[1] // 2
    row = []
    for k in range(chips):
        row += [pos[k][:, :half], pos[-k % chips][:, half:]]
    out[0:1] = jnp.concatenate(row, axis=1)
    g = lax.axis_index("grp")
    row = jnp.concatenate([n[pl.ds(g, 1)] for n in neg], axis=1)
    out[1:2, : row.shape[1]] = row


def is_here(ids, own_rows):
    here = None
    for k in range(lax.axis_size("grp")):
        low = jnp.minimum(first_of(k, 0, own_rows), first_of(k, 1, own_rows))
        hit = (ids >= low) & (ids < low + 2 * own_rows)
        here = hit if here is None else here | hit
    return here


def hits(ids, first, block):
    lane = lax.broadcasted_iota(jnp.int32, (ids.shape[0], block.shape[0]), 1)
    return ((ids - first) == lane).astype(BF16)


def pick_kernel(plan, own_rows, each, slots, scale, own_ref, other_ref, *refs):
    n = len(plan)
    blocks, refs = refs[:n], refs[n:]
    base_ref = None
    if slots is not None:
        base_ref, refs = refs[0], refs[1:]
    if not slots:
        pos_ref, row_ref = refs
        pick_rows(plan, own_rows, each, own_ref, other_ref, blocks, base_ref, [pos_ref], row_ref, 0)
        return
    before, zs = refs[0], refs[1 : 1 + slots]
    pos_ref, row_ref, logit_ref = refs[1 + slots :]
    at = before.shape[0]
    row_ref[:at] = before[...]
    pick_rows(plan, own_rows, each, own_ref, other_ref, blocks, base_ref, [pos_ref], row_ref, at)
    logits = 0.0
    width = row_ref.shape[1]
    step = chunk_of(width)
    for c in range(0, width, step):
        cols = slice(c, c + step)
        z = jnp.concatenate([z[:, cols] for z in zs], axis=0)
        logits = logits + dot(row_ref[:, cols], z, 1, 1)
    logit_ref[...] = scale * logits


def pick_rows(plan, own_rows, each, own_ref, other_ref, blocks, base_ref, pos_refs, row_ref, at):
    users = own_ref.shape[1]
    ids = column(own_ref[0:1])
    many = each * lax.axis_size("grp")
    neg = [column(r[1:2, :many]) for r in (own_ref, other_ref)]
    firsts = [first_of(k, side, own_rows) + row for side, k, row in plan]
    picks = [hits(ids, f, block) for f, block in zip(firsts, blocks)]
    owners = list(dict.fromkeys((side, k) for side, k, _ in plan))
    neg_picks = [
        hits(neg[side][k * each : (k + 1) * each], f, block)
        for (side, k, _), f, block in zip(plan, firsts, blocks)
    ]
    width = blocks[0].shape[1]
    step = chunk_of(width)
    cut = users // len(pos_refs)
    for c in range(0, width, step):
        cols = slice(c, c + step)
        rows = sum(dot(p, block[:, cols]) for p, block in zip(picks, blocks))
        if base_ref is not None:
            rows = rows + base_ref[:, cols].astype(F32)
        rows = rows.astype(BF16)
        for k, pos_ref in enumerate(pos_refs):
            pos_ref[:, cols] = rows[k * cut : (k + 1) * cut]
        for o, owner in enumerate(owners):
            mine = [n for n, (side, k, _) in enumerate(plan) if (side, k) == owner]
            got = sum(dot(neg_picks[n], blocks[n][:, cols]) for n in mine)
            row_ref[at + o * each : at + (o + 1) * each, cols] = got.astype(BF16)


def scores(scale, z_of, neg_ref, done, pos_refs, here, logit_ref, pos_out):
    width = neg_ref.shape[1]
    step = chunk_of(width)
    lanes = min(width, 128)
    slot = pos_refs[0].shape[0]
    skip = 0 if done is None else done.shape[0]
    logits = 0.0
    pos = [jnp.zeros((slot, lanes), F32) for _ in pos_refs]
    for c in range(0, width, step):
        cols = slice(c, c + step)
        z = z_of(cols)
        logits = logits + dot(neg_ref[skip:, cols], z, 1, 1)
        for k, ref in enumerate(pos_refs):
            prod = z[k * slot : (k + 1) * slot].astype(F32) * ref[:, cols].astype(F32)
            for d in range(0, step, lanes):
                pos[k] = pos[k] + prod[:, d : d + lanes]
    logits = logits * scale
    if done is not None:
        logits = jnp.concatenate([done[...], logits], axis=0)
    pos = [scale * jnp.sum(jnp.transpose(p), axis=0, keepdims=True) for p in pos]
    pos = pos[0] if len(pos) == 1 else jnp.concatenate(pos, axis=1)
    top = jnp.max(logits, axis=0, keepdims=True)
    top = jnp.where(here, jnp.maximum(top, pos), top)
    total = jnp.sum(jnp.exp(logits - top), axis=0, keepdims=True)
    total = total + jnp.where(here, jnp.exp(pos - top), 0.0)
    logit_ref[...] = logits
    pos_out[...] = pos
    return top, total


def main_kernel(plan, own_rows, each, slots, scale, own_ref, other_ref, base_ref, *refs):
    n = len(plan)
    early, done = refs[:2], refs[2]
    blocks = refs[3 : 3 + n]
    zs = refs[3 + n : 3 + n + slots]
    rest = refs[3 + n + slots :]
    pos_refs, (neg_out, logit_ref, pos_out, stat_ref) = rest[: slots + 1], rest[slots + 1 :]
    at = 0
    for e in early:
        neg_out[at : at + e.shape[0]] = e[...]
        at += e.shape[0]
    pick_rows(plan, own_rows, each, own_ref, other_ref, blocks, base_ref, pos_refs, neg_out, at)

    def z_of(cols):
        return jnp.concatenate([z[:, cols] for z in zs], axis=0)

    users = slots * pos_refs[0].shape[0]
    here = is_here(own_ref[0:1, :users], own_rows)
    top, total = scores(scale, z_of, neg_out, done, pos_refs[:slots], here, logit_ref, pos_out)
    stat_ref[0:1] = top
    stat_ref[1:2] = total


def tail_kernel(own_rows, scale, own_ref, neg_ref, pos_ref, z_ref, stat_in, *refs):
    logit_ref, pos_out, stat_ref = refs

    def z_of(cols):
        return z_ref[:, cols]

    slot = pos_ref.shape[0]
    users = own_ref.shape[1]
    here = is_here(own_ref[0:1, users - slot :], own_rows)
    top, total = scores(scale, z_of, neg_ref, None, [pos_ref], here, logit_ref, pos_out)
    stat_ref[:, : users - slot] = stat_in[...]
    stat_ref[0:1, users - slot :] = top
    stat_ref[1:2, users - slot :] = total


def join_kernel(*refs):
    out = refs[-1]
    at = 0
    for r in refs[:-1]:
        out[at : at + r.shape[0]] = r[...]
        at += r.shape[0]


def slot_total(stats, chips, k, slot):
    half = slot // 2
    tops, totals = [], []
    for s in range(chips):
        up = (k - s) % chips * slot
        down = (k + s) % chips * slot + half
        stat = jnp.concatenate(
            [stats[s][:, up : up + half], stats[s][:, down : down + half]], axis=1
        )
        tops.append(stat[0:1])
        totals.append(stat[1:2])
    peak = functools.reduce(jnp.maximum, tops)
    return peak + jnp.log(sum(t * jnp.exp(m - peak) for m, t in zip(tops, totals)))


def slot_weights(stats, chips, k, slot, logit, pos, here):
    log_total = slot_total(stats, chips, k, slot)
    prob = jnp.exp(logit - log_total).astype(BF16)
    weight = jnp.where(here, jnp.exp(pos - log_total) - 1.0, 0.0)
    return prob, weight


def slot_grad(scale, prob, weight, neg_ref, pos_ref, up_ref, down_ref):
    slot, width = pos_ref.shape
    half = slot // 2
    tall = jnp.transpose(jnp.broadcast_to(weight, (128, slot)))[:, 0:1]
    prob = jnp.transpose(prob.astype(F32)).astype(BF16)
    step = chunk_of(width)
    for c in range(0, width, step):
        cols = slice(c, c + step)
        grad = dot(prob, neg_ref[:, cols]) + tall * pos_ref[:, cols].astype(F32)
        grad = scale * grad
        up_ref[:, cols] = grad[:half].astype(up_ref.dtype)
        down_ref[:, cols] = grad[half:].astype(down_ref.dtype)


def lead_kernel(chips, own_rows, scale, order, each, own_in, logit_ref, pos_ref, *refs):
    logit_t, pos_t, neg_ref, rows_ref = refs[:4]
    stats, refs = refs[4 : 4 + chips], refs[4 + chips :]
    up_ref, down_ref, own_ref, other_ref, weight_ref, all_ref = refs
    slot = rows_ref.shape[0]
    mine = own_ref.shape[0]
    for k in range(chips):
        lanes = slice(k * slot, (k + 1) * slot)
        last = k == chips - 1
        logit = logit_t[...] if last else logit_ref[:, lanes]
        pos = pos_t[...] if last else pos_ref[:, lanes]
        here = is_here(own_in[0:1, lanes], own_rows)
        prob, weight = slot_weights(stats, chips, k, slot, logit, pos, here)
        weight_ref[:, lanes] = weight
        all_ref[:, lanes] = prob
        other_ref[mine:, lanes] = jnp.broadcast_to(weight, (16, slot)).astype(BF16)
        for n, (side, owner) in enumerate(order):
            to = other_ref if side else own_ref
            to[owner * each : (owner + 1) * each, lanes] = prob[n * each : (n + 1) * each]
        if k == 1:
            slot_grad(scale, prob, weight, neg_ref, rows_ref, up_ref, down_ref)


def rest_kernel(chips, scale, all_ref, weight_ref, neg_ref, *refs):
    rows, parts = refs[: chips - 1], refs[chips - 1 :]
    slot = rows[0].shape[0]
    others = [k for k in range(chips) if k != 1]
    for at, k in enumerate(others):
        lanes = slice(k * slot, (k + 1) * slot)
        prob, weight = all_ref[:, lanes], weight_ref[:, lanes]
        slot_grad(scale, prob, weight, neg_ref, rows[at], parts[2 * at], parts[2 * at + 1])


def item_kernel(scale, k, each, own_in, prob_own, weight_own, z_own, other_in, prob_other, z_other, *outs):
    own_rows = sum(o.shape[0] for o in outs)
    width = outs[0].shape[1]
    first = first_of(k, 0, own_rows)
    owner = slice(k * each, (k + 1) * each)
    neg = own_in[1:2, owner] - first
    pick = lax.broadcasted_iota(jnp.int32, (own_rows, each), 0) == neg
    pick = pick.astype(F32).astype(BF16)
    mine = prob_own.shape[0]
    weights = []
    for ids_ref, prob_ref, weight in (
        (own_in, prob_own, weight_own[...]),
        (other_in, prob_other, prob_other[mine : mine + 1].astype(F32)),
    ):
        ids = ids_ref[0:1] - first
        row = lax.broadcasted_iota(jnp.int32, (own_rows, ids.shape[1]), 0)
        w = dot(pick, prob_ref[owner]) + jnp.where(row == ids, weight, 0.0)
        weights.append(w.astype(BF16))
    step = chunk_of(width)
    for c in range(0, width, step):
        cols = slice(c, c + step)
        grad = scale * sum(dot(w, z[:, cols]) for w, z in zip(weights, (z_own, z_other)))
        at = 0
        for o in outs:
            o[:, cols] = grad[at : at + o.shape[0]].astype(o.dtype)
            at += o.shape[0]


def finish_kernel(up_ref, up_in_ref, down_ref, down_in_ref, hidden_ref, w_ref, out_ref):
    grad = [a[...] + b[...].astype(F32) for a, b in ((up_ref, up_in_ref), (down_ref, down_in_ref))]
    hidden = hidden_ref[...]
    s = jax.nn.sigmoid(hidden)
    slope = s * (1.0 + hidden * (1.0 - s))
    grad = (jnp.concatenate(grad, axis=0) * slope).astype(BF16)
    step = chunk_of(w_ref.shape[0])
    for c in range(0, w_ref.shape[0], step):
        cols = slice(c, c + step)
        out_ref[:, cols] = dot(grad, w_ref[:, cols]).astype(BF16)


def flip_kernel(w_ref, out_ref):
    step = chunk_of(w_ref.shape[0])
    for r in range(0, w_ref.shape[0], step):
        out_ref[:, r : r + step] = jnp.transpose(w_ref[r : r + step])


def ring_shift(x, step, chips):
    perm = [
        (chip * 2 + core, (chip + step) % chips * 2 + core)
        for chip in range(chips)
        for core in range(2)
    ]
    return lax.ppermute(x, "mem", perm)


def core_swap(x, members):
    return lax.ppermute(x, "mem", [(m, m ^ 1) for m in range(members)])


def group_swap(x, bits, groups):
    return lax.ppermute(x, "grp", [(g, g ^ bits) for g in range(groups)])


def low_bit(k):
    return k & -k


def on_device(user_rows, projection, item_table, positive, negatives):
    groups = lax.axis_size("grp")
    members = lax.axis_size("mem")
    chips = members // 2
    rows_here, width = user_rows.shape
    half = rows_here // 2
    users = chips * rows_here
    own_rows = item_table.shape[0]
    mid = own_rows // 2
    neg_rows = negatives.shape[1]
    scale = 4.0 / math.sqrt(width)
    single = [k for k in range(1, groups) if low_bit(k) == k]
    double = [k for k in range(1, groups) if low_bit(k) != k]

    block = {0: [(0, item_table)]}
    for k in single:
        block[k] = [(0, group_swap(item_table, k, groups))]
    x_up, x_down = user_rows[:half], user_rows[half:]
    z_slots = []
    for k in range(chips):
        if k:
            x_up = ring_shift(x_up, 1, chips)
            x_down = ring_shift(x_down, -1, chips)
        got = call(
            project_kernel,
            [((rows_here, width), BF16)] + ([] if k else [((rows_here, width), F32)]),
            0,
            [x_up, x_down, projection],
            2 * rows_here * width * width,
        )
        z_slots.append(got[0])
        if not k:
            hidden = got[1]
    row = positive[None]
    ids_in = [row] + [ring_shift(row, k, chips) for k in range(1, chips)]
    neg_in = [negatives] + [group_swap(negatives, k, groups) for k in range(1, groups)]
    (own,) = call(
        functools.partial(ids_kernel, chips), [((2, users), jnp.int32)], 0, ids_in + neg_in, users
    )
    other = core_swap(own, members)
    for k in double:
        low = low_bit(k)
        rest = k ^ low
        block[k] = [
            (0, group_swap(block[rest][0][1][:mid], low, groups)),
            (mid, group_swap(block[low][0][1][mid:], rest, groups)),
        ]

    def stage(ks):
        plan, rows = [], []
        for side in range(2):
            for k in ks:
                for at, piece in block[k]:
                    plan.append((side, k, at))
                    rows.append(core_swap(piece, members) if side else piece)
        return tuple(plan), rows

    slots = chips - 1
    lanes = slots * rows_here
    negs = 2 * groups * neg_rows

    def pick(plan, rows, extra, slots, more):
        return call(
            functools.partial(pick_kernel, plan, own_rows, neg_rows, slots, scale),
            [((users, width), BF16)] + more,
            0,
            [own, other] + rows + extra,
            2 * users * width * own_rows * len(rows),
        )

    plan, rows = stage([0])
    order = [(side, k) for side, k, _ in plan]
    base, neg_first = pick(plan, rows, [], None, [((len(order) * neg_rows, width), BF16)])
    plan, rows = stage(single)
    order += [(side, k) for side, k, _ in plan]
    early = len(order) * neg_rows
    base, neg_early, logits_early = pick(
        plan,
        rows,
        [base, neg_first] + z_slots[:slots],
        slots,
        [((early, width), BF16), ((early, lanes), F32)],
    )
    plan, rows = stage(double)
    cut = len(plan) // 2
    late = list(dict.fromkeys((side, k) for side, k, _ in plan))
    order += late
    base, neg_late = pick(
        plan[:cut], rows[:cut], [base], 0, [((len(late) // 2 * neg_rows, width), BF16)]
    )
    out = call(
        functools.partial(main_kernel, plan[cut:], own_rows, neg_rows, slots, scale),
        [((rows_here, width), BF16)] * chips
        + [
            ((negs, width), BF16),
            ((negs, lanes), F32),
            ((1, lanes), F32),
            ((2, lanes), F32),
        ],
        0,
        [own, other, base, neg_early, neg_late, logits_early] + rows[cut:] + z_slots[:slots],
        2 * users * width * mid * cut + 2 * users * negs * width,
    )
    pos_rows, (neg_all, logits, pos, stat) = out[:chips], out[chips:]
    logits_t, pos_t, stat = call(
        functools.partial(tail_kernel, own_rows, scale),
        [((negs, rows_here), F32), ((1, rows_here), F32), ((2, users), F32)],
        0,
        [own, neg_all, pos_rows[-1], z_slots[-1], stat],
        2 * rows_here * negs * width,
    )
    stats = [stat] + [ring_shift(stat, k, chips) for k in range(1, chips)]
    (z_all,) = call(join_kernel, [((users, width), BF16)], 0, z_slots, users * width)
    z_other = core_swap(z_all, members)
    mine = groups * neg_rows
    part = [None] * chips
    out = call(
        functools.partial(lead_kernel, chips, own_rows, scale, tuple(order), neg_rows),
        [((half, width), BF16)] * 2
        + [
            ((mine, users), BF16),
            ((mine + 16, users), BF16),
            ((1, users), F32),
            ((negs, users), BF16),
        ],
        0,
        [own, logits, pos, logits_t, pos_t, neg_all, pos_rows[1]] + stats,
        2 * rows_here * negs * width,
    )
    part[1] = out[:2]
    prob, prob_out, weight, prob_all = out[2:]
    prob_in = core_swap(prob_out, members)
    others = [k for k in range(chips) if k != 1]
    out = call(
        functools.partial(rest_kernel, chips, scale),
        [((half, width), BF16 if k else F32) for k in others for _ in range(2)],
        0,
        [prob_all, weight, neg_all] + [pos_rows[k] for k in others],
        2 * users * negs * width,
    )
    for n, k in enumerate(others):
        part[k] = out[2 * n : 2 * n + 2]

    def item_part(k, kinds):
        return call(
            functools.partial(item_kernel, scale, k, neg_rows),
            [((n, width), t) for n, t in kinds],
            0,
            [own, prob, weight, z_all, other, prob_in, z_other],
            4 * own_rows * users * width,
        )

    def ring_sum(side, step):
        moving = part[1][side]
        for k in range(2, chips):
            moving = ring_shift(moving, step, chips)
            moving = (part[k][side].astype(F32) + moving.astype(F32)).astype(BF16)
        return ring_shift(moving, step, chips)

    up_in = ring_sum(0, 1)
    down_in = ring_sum(1, -1)

    sums = {}
    for k in double + single:
        sums[k] = item_part(k, [(mid, BF16), (mid, BF16)])
    (total,) = item_part(0, [(own_rows, F32)])
    for k in double:
        low = low_bit(k)
        rest = k ^ low
        a = group_swap(sums[k][0], low, groups)
        b = group_swap(sums[k][1], rest, groups)
        sums[rest] = [(sums[rest][0].astype(F32) + a.astype(F32)).astype(BF16), sums[rest][1]]
        sums[low] = [sums[low][0], (sums[low][1].astype(F32) + b.astype(F32)).astype(BF16)]
    got = {}
    for k in single:
        got[k] = [group_swap(piece, k, groups) for piece in sums[k]]
    item_grad = total + sum(jnp.concatenate(got[k]).astype(F32) for k in single)
    (flipped,) = call(flip_kernel, [((width, width), BF16)], 0, [projection], width)
    (user_grad,) = call(
        finish_kernel,
        [((rows_here, width), BF16)],
        0,
        [part[0][0], up_in, part[0][1], down_in, hidden, flipped],
        2 * rows_here * width * width,
    )
    return (user_grad, item_grad)


def solution(mesh):
    owners = ("grp", "mem")

    return jax.shard_map(
        on_device,
        mesh=mesh,
        in_specs=(P(owners, None), P(), P(owners, None), P(owners), P(None, owners)),
        out_specs=(P(owners, None), P(owners, None)),
        check_vma=False,
    )
```

```python
import functools
import math

import jax
import jax.numpy as jnp
from jax import lax
from jax.experimental import pallas as pl
from jax.experimental.pallas import tpu as pltpu
from jax.sharding import PartitionSpec as P


F32 = jnp.float32
BF16 = jnp.bfloat16
VMEM_LIMIT = 60 * 1024 * 1024
SPARE = 6 * 1024 * 1024
VM = pl.BlockSpec(memory_space=pltpu.VMEM)
SM = pl.BlockSpec(memory_space=pltpu.SMEM)


def dot(a, b, ca=1, cb=0):
    return lax.dot_general(a, b, (((ca,), (cb,)), ((), ())), preferred_element_type=F32)


def chunk_of(width):
    return width if width < 256 else 256


def cost(flops, nbytes):
    return pl.CostEstimate(flops=int(flops), bytes_accessed=int(nbytes), transcendentals=0)


def size_of(shape, dtype):
    return math.prod(shape) * jnp.dtype(dtype).itemsize


def call(kernel, outs, n_smem, args, flops):
    nbytes = sum(size_of(x.shape, x.dtype) for x in args[n_smem:])
    nbytes += sum(size_of(s, t) for s, t in outs)
    return pl.pallas_call(
        kernel,
        out_shape=[jax.ShapeDtypeStruct(s, t) for s, t in outs],
        in_specs=[SM] * n_smem + [VM] * (len(args) - n_smem),
        out_specs=[VM] * len(outs),
        compiler_params=pltpu.CompilerParams(
            vmem_limit_bytes=min(VMEM_LIMIT, nbytes * 3 // 2 + SPARE)
        ),
        cost_estimate=cost(flops, nbytes),
    )(*args)


def project_kernel(x_up, x_down, w_ref, z_ref, *hidden_ref):
    x = jnp.concatenate([x_up[...], x_down[...]], axis=0)
    width = w_ref.shape[1]
    step = chunk_of(width)
    for c in range(0, width, step):
        cols = slice(c, c + step)
        hidden = dot(x, w_ref[:, cols])
        if hidden_ref:
            hidden_ref[0][:, cols] = hidden
        z_ref[:, cols] = (hidden * jax.nn.sigmoid(hidden)).astype(BF16)


def first_of(k, side, own_rows):
    g, m = lax.axis_index("grp"), lax.axis_index("mem")
    return ((g ^ k) * lax.axis_size("mem") + (m ^ side)) * own_rows


def column(row):
    tall = jnp.broadcast_to(row.astype(F32), (128, row.shape[1]))
    return jnp.transpose(tall)[:, 0:1].astype(jnp.int32)


def ids_kernel(chips, *refs):
    pos, neg, out = refs[:chips], refs[chips:-1], refs[-1]
    half = pos[0].shape[1] // 2
    row = []
    for k in range(chips):
        row += [pos[k][:, :half], pos[-k % chips][:, half:]]
    out[0:1] = jnp.concatenate(row, axis=1)
    g = lax.axis_index("grp")
    row = jnp.concatenate([n[pl.ds(g, 1)] for n in neg], axis=1)
    out[1:2, : row.shape[1]] = row


def is_here(ids, own_rows):
    here = None
    for k in range(lax.axis_size("grp")):
        low = jnp.minimum(first_of(k, 0, own_rows), first_of(k, 1, own_rows))
        hit = (ids >= low) & (ids < low + 2 * own_rows)
        here = hit if here is None else here | hit
    return here


def hits(ids, first, block):
    lane = lax.broadcasted_iota(jnp.int32, (ids.shape[0], block.shape[0]), 1)
    return ((ids - first) == lane).astype(BF16)


def pick_kernel(plan, own_rows, each, slots, scale, own_ref, other_ref, *refs):
    n = len(plan)
    blocks, refs = refs[:n], refs[n:]
    base_ref = None
    if slots is not None:
        base_ref, refs = refs[0], refs[1:]
    if not slots:
        pos_ref, row_ref = refs
        pick_rows(plan, own_rows, each, own_ref, other_ref, blocks, base_ref, [pos_ref], row_ref, 0)
        return
    before, zs = refs[0], refs[1 : 1 + slots]
    pos_ref, row_ref, logit_ref = refs[1 + slots :]
    at = before.shape[0]
    row_ref[:at] = before[...]
    pick_rows(plan, own_rows, each, own_ref, other_ref, blocks, base_ref, [pos_ref], row_ref, at)
    logits = 0.0
    width = row_ref.shape[1]
    step = chunk_of(width)
    for c in range(0, width, step):
        cols = slice(c, c + step)
        z = jnp.concatenate([z[:, cols] for z in zs], axis=0)
        logits = logits + dot(row_ref[:, cols], z, 1, 1)
    logit_ref[...] = scale * logits


def pick_rows(plan, own_rows, each, own_ref, other_ref, blocks, base_ref, pos_refs, row_ref, at):
    users = own_ref.shape[1]
    ids = column(own_ref[0:1])
    many = each * lax.axis_size("grp")
    neg = [column(r[1:2, :many]) for r in (own_ref, other_ref)]
    firsts = [first_of(k, side, own_rows) + row for side, k, row in plan]
    picks = [hits(ids, f, block) for f, block in zip(firsts, blocks)]
    owners = list(dict.fromkeys((side, k) for side, k, _ in plan))
    neg_picks = [
        hits(neg[side][k * each : (k + 1) * each], f, block)
        for (side, k, _), f, block in zip(plan, firsts, blocks)
    ]
    width = blocks[0].shape[1]
    step = chunk_of(width)
    cut = users // len(pos_refs)
    for c in range(0, width, step):
        cols = slice(c, c + step)
        rows = sum(dot(p, block[:, cols]) for p, block in zip(picks, blocks))
        if base_ref is not None:
            rows = rows + base_ref[:, cols].astype(F32)
        rows = rows.astype(BF16)
        for k, pos_ref in enumerate(pos_refs):
            pos_ref[:, cols] = rows[k * cut : (k + 1) * cut]
        for o, owner in enumerate(owners):
            mine = [n for n, (side, k, _) in enumerate(plan) if (side, k) == owner]
            got = sum(dot(neg_picks[n], blocks[n][:, cols]) for n in mine)
            row_ref[at + o * each : at + (o + 1) * each, cols] = got.astype(BF16)


def scores(scale, z_of, neg_ref, done, pos_refs, here, logit_ref, pos_out):
    width = neg_ref.shape[1]
    step = chunk_of(width)
    lanes = min(width, 128)
    slot = pos_refs[0].shape[0]
    skip = 0 if done is None else done.shape[0]
    logits = 0.0
    pos = [jnp.zeros((slot, lanes), F32) for _ in pos_refs]
    for c in range(0, width, step):
        cols = slice(c, c + step)
        z = z_of(cols)
        logits = logits + dot(neg_ref[skip:, cols], z, 1, 1)
        for k, ref in enumerate(pos_refs):
            prod = z[k * slot : (k + 1) * slot].astype(F32) * ref[:, cols].astype(F32)
            for d in range(0, step, lanes):
                pos[k] = pos[k] + prod[:, d : d + lanes]
    logits = logits * scale
    if done is not None:
        logits = jnp.concatenate([done[...], logits], axis=0)
    pos = [scale * jnp.sum(jnp.transpose(p), axis=0, keepdims=True) for p in pos]
    pos = pos[0] if len(pos) == 1 else jnp.concatenate(pos, axis=1)
    top = jnp.max(logits, axis=0, keepdims=True)
    top = jnp.where(here, jnp.maximum(top, pos), top)
    total = jnp.sum(jnp.exp(logits - top), axis=0, keepdims=True)
    total = total + jnp.where(here, jnp.exp(pos - top), 0.0)
    logit_ref[...] = logits
    pos_out[...] = pos
    return top, total


def main_kernel(plan, own_rows, each, slots, scale, own_ref, other_ref, base_ref, *refs):
    n = len(plan)
    early, done = refs[:2], refs[2]
    blocks = refs[3 : 3 + n]
    zs = refs[3 + n : 3 + n + slots]
    rest = refs[3 + n + slots :]
    pos_refs, (neg_out, logit_ref, pos_out, stat_ref) = rest[: slots + 1], rest[slots + 1 :]
    at = 0
    for e in early:
        neg_out[at : at + e.shape[0]] = e[...]
        at += e.shape[0]
    pick_rows(plan, own_rows, each, own_ref, other_ref, blocks, base_ref, pos_refs, neg_out, at)

    def z_of(cols):
        return jnp.concatenate([z[:, cols] for z in zs], axis=0)

    users = slots * pos_refs[0].shape[0]
    here = is_here(own_ref[0:1, :users], own_rows)
    top, total = scores(scale, z_of, neg_out, done, pos_refs[:slots], here, logit_ref, pos_out)
    stat_ref[0:1] = top
    stat_ref[1:2] = total


def tail_kernel(own_rows, scale, own_ref, neg_ref, pos_ref, z_ref, stat_in, *refs):
    logit_ref, pos_out, stat_ref = refs

    def z_of(cols):
        return z_ref[:, cols]

    slot = pos_ref.shape[0]
    users = own_ref.shape[1]
    here = is_here(own_ref[0:1, users - slot :], own_rows)
    top, total = scores(scale, z_of, neg_ref, None, [pos_ref], here, logit_ref, pos_out)
    stat_ref[:, : users - slot] = stat_in[...]
    stat_ref[0:1, users - slot :] = top
    stat_ref[1:2, users - slot :] = total


def join_kernel(*refs):
    out = refs[-1]
    at = 0
    for r in refs[:-1]:
        out[at : at + r.shape[0]] = r[...]
        at += r.shape[0]


def slot_total(stats, chips, k, slot):
    half = slot // 2
    tops, totals = [], []
    for s in range(chips):
        up = (k - s) % chips * slot
        down = (k + s) % chips * slot + half
        stat = jnp.concatenate(
            [stats[s][:, up : up + half], stats[s][:, down : down + half]], axis=1
        )
        tops.append(stat[0:1])
        totals.append(stat[1:2])
    peak = functools.reduce(jnp.maximum, tops)
    return peak + jnp.log(sum(t * jnp.exp(m - peak) for m, t in zip(tops, totals)))


def slot_weights(stats, chips, k, slot, logit, pos, here):
    log_total = slot_total(stats, chips, k, slot)
    prob = jnp.exp(logit - log_total).astype(BF16)
    weight = jnp.where(here, jnp.exp(pos - log_total) - 1.0, 0.0)
    return prob, weight


def slot_grad(scale, prob, weight, neg_ref, pos_ref, up_ref, down_ref):
    slot, width = pos_ref.shape
    half = slot // 2
    tall = jnp.transpose(jnp.broadcast_to(weight, (128, slot)))[:, 0:1]
    prob = jnp.transpose(prob.astype(F32)).astype(BF16)
    step = chunk_of(width)
    for c in range(0, width, step):
        cols = slice(c, c + step)
        grad = dot(prob, neg_ref[:, cols]) + tall * pos_ref[:, cols].astype(F32)
        grad = scale * grad
        up_ref[:, cols] = grad[:half].astype(up_ref.dtype)
        down_ref[:, cols] = grad[half:].astype(down_ref.dtype)


def lead_kernel(chips, own_rows, scale, order, each, own_in, logit_ref, pos_ref, *refs):
    logit_t, pos_t, neg_ref, rows_ref = refs[:4]
    stats, refs = refs[4 : 4 + chips], refs[4 + chips :]
    up_ref, down_ref, own_ref, other_ref, weight_ref, all_ref = refs
    slot = rows_ref.shape[0]
    mine = own_ref.shape[0]
    for k in range(chips):
        lanes = slice(k * slot, (k + 1) * slot)
        last = k == chips - 1
        logit = logit_t[...] if last else logit_ref[:, lanes]
        pos = pos_t[...] if last else pos_ref[:, lanes]
        here = is_here(own_in[0:1, lanes], own_rows)
        prob, weight = slot_weights(stats, chips, k, slot, logit, pos, here)
        weight_ref[:, lanes] = weight
        all_ref[:, lanes] = prob
        other_ref[mine:, lanes] = jnp.broadcast_to(weight, (16, slot)).astype(BF16)
        for n, (side, owner) in enumerate(order):
            to = other_ref if side else own_ref
            to[owner * each : (owner + 1) * each, lanes] = prob[n * each : (n + 1) * each]
        if k == 1:
            slot_grad(scale, prob, weight, neg_ref, rows_ref, up_ref, down_ref)


def rest_kernel(chips, scale, all_ref, weight_ref, neg_ref, *refs):
    rows, parts = refs[: chips - 1], refs[chips - 1 :]
    slot = rows[0].shape[0]
    others = [k for k in range(chips) if k != 1]
    for at, k in enumerate(others):
        lanes = slice(k * slot, (k + 1) * slot)
        prob, weight = all_ref[:, lanes], weight_ref[:, lanes]
        slot_grad(scale, prob, weight, neg_ref, rows[at], parts[2 * at], parts[2 * at + 1])


def item_kernel(scale, k, each, more, own_in, prob_own, weight_own, z_own, *refs):
    other_in, prob_other, z_other = refs[:3]
    adds, outs = refs[3 : 3 + more], refs[3 + more :]
    own_rows = sum(o.shape[0] for o in outs)
    width = outs[0].shape[1]
    first = first_of(k, 0, own_rows)
    owner = slice(k * each, (k + 1) * each)
    neg = own_in[1:2, owner] - first
    pick = lax.broadcasted_iota(jnp.int32, (own_rows, each), 0) == neg
    pick = pick.astype(F32).astype(BF16)
    mine = prob_own.shape[0]
    weights = []
    for ids_ref, prob_ref, weight in (
        (own_in, prob_own, weight_own[...]),
        (other_in, prob_other, prob_other[mine : mine + 1].astype(F32)),
    ):
        ids = ids_ref[0:1] - first
        row = lax.broadcasted_iota(jnp.int32, (own_rows, ids.shape[1]), 0)
        w = dot(pick, prob_ref[owner]) + jnp.where(row == ids, weight, 0.0)
        weights.append(w.astype(BF16))
    step = chunk_of(width)
    for c in range(0, width, step):
        cols = slice(c, c + step)
        grad = scale * sum(dot(w, z[:, cols]) for w, z in zip(weights, (z_own, z_other)))
        if more:
            grad = grad + jnp.concatenate([a[:, cols].astype(F32) for a in adds], axis=0)
        at = 0
        for o in outs:
            o[:, cols] = grad[at : at + o.shape[0]].astype(o.dtype)
            at += o.shape[0]


def finish_kernel(up_ref, up_in_ref, down_ref, down_in_ref, hidden_ref, w_ref, out_ref):
    grad = [a[...] + b[...].astype(F32) for a, b in ((up_ref, up_in_ref), (down_ref, down_in_ref))]
    hidden = hidden_ref[...]
    s = jax.nn.sigmoid(hidden)
    slope = s * (1.0 + hidden * (1.0 - s))
    grad = (jnp.concatenate(grad, axis=0) * slope).astype(BF16)
    step = chunk_of(w_ref.shape[0])
    for c in range(0, w_ref.shape[0], step):
        cols = slice(c, c + step)
        out_ref[:, cols] = dot(grad, w_ref[:, cols]).astype(BF16)


def flip_kernel(w_ref, out_ref):
    step = chunk_of(w_ref.shape[0])
    for r in range(0, w_ref.shape[0], step):
        out_ref[:, r : r + step] = jnp.transpose(w_ref[r : r + step])


def ring_shift(x, step, chips):
    perm = [
        (chip * 2 + core, (chip + step) % chips * 2 + core)
        for chip in range(chips)
        for core in range(2)
    ]
    return lax.ppermute(x, "mem", perm)


def core_swap(x, members):
    return lax.ppermute(x, "mem", [(m, m ^ 1) for m in range(members)])


def group_swap(x, bits, groups):
    return lax.ppermute(x, "grp", [(g, g ^ bits) for g in range(groups)])


def low_bit(k):
    return k & -k


def on_device(user_rows, projection, item_table, positive, negatives):
    groups = lax.axis_size("grp")
    members = lax.axis_size("mem")
    chips = members // 2
    rows_here, width = user_rows.shape
    half = rows_here // 2
    users = chips * rows_here
    own_rows = item_table.shape[0]
    mid = own_rows // 2
    neg_rows = negatives.shape[1]
    scale = 4.0 / math.sqrt(width)
    single = [k for k in range(1, groups) if low_bit(k) == k]
    double = [k for k in range(1, groups) if low_bit(k) != k]

    block = {0: [(0, item_table)]}
    for k in single:
        block[k] = [(0, group_swap(item_table, k, groups))]
    x_up, x_down = user_rows[:half], user_rows[half:]
    z_slots = []
    for k in range(chips):
        if k:
            x_up = ring_shift(x_up, 1, chips)
            x_down = ring_shift(x_down, -1, chips)
        got = call(
            project_kernel,
            [((rows_here, width), BF16)] + ([] if k else [((rows_here, width), F32)]),
            0,
            [x_up, x_down, projection],
            2 * rows_here * width * width,
        )
        z_slots.append(got[0])
        if not k:
            hidden = got[1]
    row = positive[None]
    ids_in = [row] + [ring_shift(row, k, chips) for k in range(1, chips)]
    neg_in = [negatives] + [group_swap(negatives, k, groups) for k in range(1, groups)]
    (own,) = call(
        functools.partial(ids_kernel, chips), [((2, users), jnp.int32)], 0, ids_in + neg_in, users
    )
    other = core_swap(own, members)
    for k in double:
        low = low_bit(k)
        rest = k ^ low
        block[k] = [
            (0, group_swap(block[rest][0][1][:mid], low, groups)),
            (mid, group_swap(block[low][0][1][mid:], rest, groups)),
        ]

    def stage(ks):
        plan, rows = [], []
        for side in range(2):
            for k in ks:
                for at, piece in block[k]:
                    plan.append((side, k, at))
                    rows.append(core_swap(piece, members) if side else piece)
        return tuple(plan), rows

    slots = chips - 1
    lanes = slots * rows_here
    negs = 2 * groups * neg_rows

    def pick(plan, rows, extra, slots, more):
        return call(
            functools.partial(pick_kernel, plan, own_rows, neg_rows, slots, scale),
            [((users, width), BF16)] + more,
            0,
            [own, other] + rows + extra,
            2 * users * width * own_rows * len(rows),
        )

    plan, rows = stage([0])
    order = [(side, k) for side, k, _ in plan]
    base, neg_first = pick(plan, rows, [], None, [((len(order) * neg_rows, width), BF16)])
    plan, rows = stage(single)
    order += [(side, k) for side, k, _ in plan]
    early = len(order) * neg_rows
    base, neg_early, logits_early = pick(
        plan,
        rows,
        [base, neg_first] + z_slots[:slots],
        slots,
        [((early, width), BF16), ((early, lanes), F32)],
    )
    plan, rows = stage(double)
    cut = len(plan) // 2
    late = list(dict.fromkeys((side, k) for side, k, _ in plan))
    order += late
    base, neg_late = pick(
        plan[:cut], rows[:cut], [base], 0, [((len(late) // 2 * neg_rows, width), BF16)]
    )
    out = call(
        functools.partial(main_kernel, plan[cut:], own_rows, neg_rows, slots, scale),
        [((rows_here, width), BF16)] * chips
        + [
            ((negs, width), BF16),
            ((negs, lanes), F32),
            ((1, lanes), F32),
            ((2, lanes), F32),
        ],
        0,
        [own, other, base, neg_early, neg_late, logits_early] + rows[cut:] + z_slots[:slots],
        2 * users * width * mid * cut + 2 * users * negs * width,
    )
    pos_rows, (neg_all, logits, pos, stat) = out[:chips], out[chips:]
    logits_t, pos_t, stat = call(
        functools.partial(tail_kernel, own_rows, scale),
        [((negs, rows_here), F32), ((1, rows_here), F32), ((2, users), F32)],
        0,
        [own, neg_all, pos_rows[-1], z_slots[-1], stat],
        2 * rows_here * negs * width,
    )
    stats = [stat] + [ring_shift(stat, k, chips) for k in range(1, chips)]
    (z_all,) = call(join_kernel, [((users, width), BF16)], 0, z_slots, users * width)
    z_other = core_swap(z_all, members)
    mine = groups * neg_rows
    part = [None] * chips
    out = call(
        functools.partial(lead_kernel, chips, own_rows, scale, tuple(order), neg_rows),
        [((half, width), BF16)] * 2
        + [
            ((mine, users), BF16),
            ((mine + 16, users), BF16),
            ((1, users), F32),
            ((negs, users), BF16),
        ],
        0,
        [own, logits, pos, logits_t, pos_t, neg_all, pos_rows[1]] + stats,
        2 * rows_here * negs * width,
    )
    part[1] = out[:2]
    prob, prob_out, weight, prob_all = out[2:]
    prob_in = core_swap(prob_out, members)
    others = [k for k in range(chips) if k != 1]
    out = call(
        functools.partial(rest_kernel, chips, scale),
        [((half, width), BF16 if k else F32) for k in others for _ in range(2)],
        0,
        [prob_all, weight, neg_all] + [pos_rows[k] for k in others],
        2 * users * negs * width,
    )
    for n, k in enumerate(others):
        part[k] = out[2 * n : 2 * n + 2]

    def item_part(k, kinds, adds=()):
        return call(
            functools.partial(item_kernel, scale, k, neg_rows, len(adds)),
            [((n, width), t) for n, t in kinds],
            0,
            [own, prob, weight, z_all, other, prob_in, z_other] + list(adds),
            4 * own_rows * users * width,
        )

    def ring_sum(side, step):
        moving = part[1][side]
        for k in range(2, chips):
            moving = ring_shift(moving, step, chips)
            moving = (part[k][side].astype(F32) + moving.astype(F32)).astype(BF16)
        return ring_shift(moving, step, chips)

    up_in = ring_sum(0, 1)
    down_in = ring_sum(1, -1)

    sums = {}
    for k in double + single:
        sums[k] = item_part(k, [(mid, BF16), (mid, BF16)])
    got = {(k, n): None for k in single for n in range(2)}
    forwarded = set()
    for k in double:
        low = low_bit(k)
        rest = k ^ low
        a = group_swap(sums[k][0], low, groups)
        b = group_swap(sums[k][1], rest, groups)
        sums[rest] = [(sums[rest][0].astype(F32) + a.astype(F32)).astype(BF16), sums[rest][1]]
        sums[low] = [sums[low][0], (sums[low][1].astype(F32) + b.astype(F32)).astype(BF16)]
        forwarded |= {(rest, 0), (low, 1)}
    for k, n in got:
        got[k, n] = group_swap(sums[k][n], k, groups)
    soon = [[got[k, n] for k in single if (k, n) not in forwarded] for n in range(2)]
    last = [[got[k, n] for k in single if (k, n) in forwarded] for n in range(2)]
    (total,) = item_part(0, [(own_rows, F32)], [sum(s[1:], s[0]) for s in soon])
    item_grad = total + jnp.concatenate([sum(x.astype(F32) for x in s) for s in last])
    (flipped,) = call(flip_kernel, [((width, width), BF16)], 0, [projection], width)
    (user_grad,) = call(
        finish_kernel,
        [((rows_here, width), BF16)],
        0,
        [part[0][0], up_in, part[0][1], down_in, hidden, flipped],
        2 * rows_here * width * width,
    )
    return (user_grad, item_grad)


def solution(mesh):
    owners = ("grp", "mem")

    return jax.shard_map(
        on_device,
        mesh=mesh,
        in_specs=(P(owners, None), P(), P(owners, None), P(owners), P(None, owners)),
        out_specs=(P(owners, None), P(owners, None)),
        check_vma=False,
    )
```
